512 devices in a mesh: sub: 128 (over y, z, core), pln: 4 (over x).
Axes of the slice: x: 4, y: 8, z: 8, core: 2. Of those that a mesh axis runs over, the one named last changes fastest.
Arguments:
- labels: int32 [8, 64, 16384], P('pln', None, 'sub'), may hold values from 0 to 3
- levels: float32 [4], replicated, may hold values from 0.1 to 1
- zvec: bfloat16 [64, 8, 64, 16384], P(None, 'pln', None, 'sub'), may hold values from -1 to 1
- resid: float32 [8, 64, 16384], P('pln', None, 'sub'), may hold values from -6 to 6
Outputs:
- coarse_solution: float32 [128, 64], P('sub')
- deflated: float32 [8, 64, 16384], P('pln', None, 'sub')
The draws below stay inside these ranges and needn't reach their ends.
All inputs are finite; a program needn't handle non-finite values.
Results may differ from the reference program's by a relative error of at most 0.0003.
Values may be sent and summed in bfloat16 or wider, within the bound.
A program may use at most 128 MiB of HBM per device.

```python
import math
import jax
import jax.numpy as jnp
from jax import lax

K = 64
NLEV = 4
CITERS = 2
NY = 64
CZ = 128
NX = 8
NZ = 16384
SUBS = 128


def draw_zvec(key, part):
    mode_key = jax.random.fold_in(key, 11)
    rough_key = jax.random.fold_in(key, 12)
    modes = jax.random.truncated_normal(mode_key, -3.0, 3.0, (K, NX, NY), jnp.float32)
    rough = jax.random.uniform(rough_key, (K, NX, NY, NZ), jnp.float32, 0.5, 1.5)
    layer = jnp.arange(NZ) % CZ
    distance = jnp.minimum(layer, CZ - 1 - layer).astype(jnp.float32)
    profile = 0.5 + 1.5 * jnp.exp(-distance / 4.0)
    total = 0.0
    for position in range(CZ):
        total = total + (0.5 + 1.5 * math.exp(-min(position, CZ - 1 - position) / 4.0)) ** 2
    factor = 1.0 / math.sqrt(total * NX * NY)
    return (modes[..., None] * profile * rough * factor).astype(jnp.bfloat16)


def place_ends(result, rng, low, top_value):
    longest = result.shape.index(max(result.shape))
    spots = []
    for shift in (0, 1):
        where = [jax.random.randint(jax.random.fold_in(rng, axis), (), 0, length) for axis, length in enumerate(result.shape)]
        where[longest] = (where[longest] + shift) % result.shape[longest]
        spots.append(tuple(where))
    return result.at[spots[0]].set(low).at[spots[1]].set(top_value)


def level_of(rng, shape, split, smallest, top_value):
    level = 1.0
    for dim, blocks in split:
        heights = jax.random.uniform(jax.random.fold_in(jax.random.fold_in(rng, 6), dim), (blocks,), jnp.float32, smallest / len(split), top_value / len(split))
        level = level * jnp.repeat(jnp.exp(heights), shape[dim] // blocks).reshape((-1,) + (1,) * (len(shape) - 1 - dim))
    return level


def noise(stream_key, extent, spread, reach, split=(), kind=jnp.bfloat16):
    result = jax.random.normal(stream_key, extent, jnp.float32) * spread
    if len(split) > 0:
        result = level_of(stream_key, extent, split, -0.22, 0.18) * result
    return jnp.clip(result, min=-reach, max=reach).astype(kind)


def setup_inputs(seed: int = 0) -> dict:
    key_of = jax.random.split(jax.random.key(seed), 5)
    labels = place_ends(jax.random.randint(key_of[0], (NX, NY, NZ), 0, NLEV), jax.random.fold_in(key_of[0], 1), 0, NLEV - 1).astype(jnp.int32)
    levels = jnp.clip(jnp.exp(jax.random.uniform(key_of[1], (NLEV,), jnp.float32, math.log(0.1), math.log(1.0))), 0.1, 1.0)
    zvec = draw_zvec(jax.random.fold_in(key_of[4], 71), 0)
    resid = noise(key_of[3], (NX, NY, NZ), 1.0, 6.0, ((0, 4), (2, 128)), jnp.float32)
    return dict(labels=labels, levels=levels, zvec=zvec, resid=resid)


PRECISE = lax.Precision.HIGHEST


def harmonic(left_value, right_value):
    return 2.0 * left_value * right_value / (left_value + right_value)


def coefficients(labels, levels):
    weighted = jnp.zeros(labels.shape, jnp.float32)
    for level_index in range(levels.shape[0]):
        weighted = weighted + jnp.where(labels == level_index, levels[level_index], 0.0)
    return weighted


def apply_yz(fine_field, weights, z_below, z_above):
    zero_plane = jnp.zeros_like(fine_field[..., :1, :])
    below_y = jnp.concatenate([zero_plane, fine_field[..., :-1, :]], axis=-2)
    above_y = jnp.concatenate([fine_field[..., 1:, :], zero_plane], axis=-2)
    below_z = jnp.concatenate([z_below, fine_field[..., :-1]], axis=-1)
    above_z = jnp.concatenate([fine_field[..., 1:], z_above], axis=-1)
    return (weights[2] * (fine_field - below_y) + weights[3] * (fine_field - above_y)
            + weights[4] * (fine_field - below_z) + weights[5] * (fine_field - above_z))


def apply_full(fine_field, weights, x_below, x_above, z_below, z_above):
    below_x = jnp.concatenate([x_below, fine_field[..., :-1, :, :]], axis=-3)
    above_x = jnp.concatenate([fine_field[..., 1:, :, :], x_above], axis=-3)
    return (weights[0] * (fine_field - below_x) + weights[1] * (fine_field - above_x)
            + apply_yz(fine_field, weights, z_below, z_above))


def face_weights(density_coef):
    pad_x = jnp.pad(density_coef, ((1, 1), (0, 0), (0, 0)), mode="edge")
    pad_y = jnp.pad(density_coef, ((0, 0), (1, 1), (0, 0)), mode="edge")
    return (harmonic(density_coef, pad_x[:-2]), harmonic(density_coef, pad_x[2:]),
            harmonic(density_coef, pad_y[:, :-2]), harmonic(density_coef, pad_y[:, 2:]),
            harmonic(density_coef, jnp.roll(density_coef, 1, axis=2)),
            harmonic(density_coef, jnp.roll(density_coef, -1, axis=2)))


def coarse_apply(diag_blocks, upper_blocks, direction):
    ahead_term = jnp.roll(direction, -1, axis=0)
    behind_term = jnp.roll(direction, 1, axis=0)
    upper_behind = jnp.roll(upper_blocks, 1, axis=0)
    return (jnp.einsum("skl,sl->sk", diag_blocks, direction, precision=PRECISE)
            + jnp.einsum("skl,sl->sk", upper_blocks, ahead_term, precision=PRECISE)
            + jnp.einsum("slk,sl->sk", upper_behind, behind_term, precision=PRECISE))


def reference(labels, levels, zvec, resid):
    density_coef = coefficients(labels, levels)
    weights = face_weights(density_coef)

    def slab_terms(slab_index):
        start = (slab_index * CZ).astype(jnp.int32)
        next_start = (((slab_index + 1) % SUBS) * CZ).astype(jnp.int32)
        own_modes = lax.dynamic_slice_in_dim(zvec, start, CZ, axis=3).astype(jnp.float32)
        first_layer = lax.dynamic_slice_in_dim(zvec, next_start, 1, axis=3).astype(jnp.float32)
        slab_weights = tuple(lax.dynamic_slice_in_dim(weight_field, start, CZ, axis=2) for weight_field in weights)
        slab_resid = lax.dynamic_slice_in_dim(resid, start, CZ, axis=2)
        x_zero = jnp.zeros_like(own_modes[:, :1])
        z_zero = jnp.zeros_like(own_modes[..., :1])
        stencil_image = apply_full(own_modes, slab_weights, x_zero, x_zero, z_zero, z_zero)
        flat_modes = own_modes.reshape(K, -1)
        diag_block = jnp.dot(flat_modes, stencil_image.reshape(K, -1).T, precision=PRECISE)
        edge_rows = (own_modes[..., -1] * slab_weights[5][..., -1]).reshape(K, -1)
        upper_block = -jnp.dot(edge_rows, first_layer.reshape(K, -1).T, precision=PRECISE)
        slab_rhs = jnp.dot(flat_modes, slab_resid.reshape(-1), precision=PRECISE)
        return diag_block, upper_block, slab_rhs

    diag_blocks, upper_blocks, coarse_rhs = lax.map(slab_terms, jnp.arange(SUBS, dtype=jnp.int32))

    solution = jnp.zeros_like(coarse_rhs)
    remain = coarse_rhs
    direction = coarse_rhs
    norm_now = jnp.sum(remain * remain)
    for iteration in range(CITERS):
        stencil_image = coarse_apply(diag_blocks, upper_blocks, direction)
        step_size = norm_now / jnp.sum(direction * stencil_image)
        solution = solution + step_size * direction
        remain = remain - step_size * stencil_image
        norm_next = jnp.sum(remain * remain)
        direction = remain + (norm_next / norm_now) * direction
        norm_now = norm_next

    def slab_field(slab_index):
        start = (slab_index * CZ).astype(jnp.int32)
        own_modes = lax.dynamic_slice_in_dim(zvec, start, CZ, axis=3).astype(jnp.float32)
        return jnp.dot(solution[slab_index], own_modes.reshape(K, -1), precision=PRECISE).reshape(NX, NY, CZ)

    slabs = lax.map(slab_field, jnp.arange(SUBS, dtype=jnp.int32))
    fine_field = jnp.moveaxis(slabs, 0, 2).reshape(NX, NY, NZ)
    x_zero = jnp.zeros_like(fine_field[:1])
    stencil_image = apply_full(fine_field, weights, x_zero, x_zero, fine_field[..., -1:], fine_field[..., :1])
    return solution, resid - stencil_image
```

```python
import functools
import math

import jax
import jax.numpy as jnp
from jax import lax
from jax.experimental import pallas as pl
from jax.experimental.pallas import tpu as pltpu
from jax.sharding import PartitionSpec as P

MESH = pl.DeviceIdType.MESH
PRECISE = lax.Precision.HIGHEST
ZCHUNKS = 4
STEP = 4


def harmonic(left_value, right_value):
    return 2.0 * left_value * right_value / (left_value + right_value)


def kernel(
    sides,
    levels,
    labels_hbm,
    z_hbm,
    resid_hbm,
    sol_ref,
    defl_ref,
    z,
    lab,
    res,
    lab_x,
    lab_z,
    field,
    field_x,
    field_z,
    spread,
    part,
    rows,
    sums,
    wts,
    load_sem,
    side_send,
    side_recv,
    row_send,
    row_recv,
    sum_send,
    sum_recv,
):
    ny, nz, npln = sides
    nsub = ny * nz * 2
    modes, planes, height, depth = z.shape
    sub = lax.axis_index("sub")
    pln = lax.axis_index("pln")
    core = sub % 2
    zc = (sub // 2) % nz
    yc = sub // (2 * nz)
    first_pln = pln == 0
    last_pln = pln == npln - 1

    per = modes // ZCHUNKS
    small = (
        pltpu.make_async_copy(labels_hbm, lab, load_sem.at[0]),
        pltpu.make_async_copy(resid_hbm, res, load_sem.at[1]),
    )
    big = [
        pltpu.make_async_copy(
            z_hbm.at[pl.ds(i * per, per)], z.at[pl.ds(i * per, per)], load_sem.at[2 + i]
        )
        for i in range(ZCHUNKS)
    ]
    for copy in small:
        copy.start()
    for copy in big:
        copy.start()

    def group(stage):
        if stage == 0:
            count, me = npln * 2, pln * 2 + core
        elif stage == 1:
            count, me = nz, zc
        else:
            count, me = ny, yc
        peers = []
        for off in range(1, count):
            other = (me + off) % count
            if stage == 0:
                peers.append((sub - core + other % 2, other // 2))
            elif stage == 1:
                peers.append(((yc * nz + other) * 2 + core, pln))
            else:
                peers.append(((other * nz + zc) * 2 + core, pln))
        return count, me, peers

    groups = [group(stage) for stage in range(3)]
    ahead = ((sub + 1) % nsub, pln)
    behind = ((sub + nsub - 1) % nsub, pln)
    right = (sub, (pln + 1) % npln)
    left = (sub, (pln + npln - 1) % npln)
    far = ((sub + 2 * core + nsub - 1) % nsub, pln)

    barrier = pltpu.get_barrier_semaphore()
    total = 1
    pl.semaphore_signal(barrier, inc=1, device_id=far, device_id_type=MESH)
    for _, _, peers in groups:
        for peer in peers:
            pl.semaphore_signal(barrier, inc=1, device_id=peer, device_id_type=MESH)
            total += 1
    pl.semaphore_wait(barrier, total)

    pending = []

    def side_copies(which, src, dst_x, dst_z):
        copies = []
        for side, (piece, target, place) in enumerate(
            (
                (src.at[planes - 1], right, dst_x.at[0]),
                (src.at[0], left, dst_x.at[1]),
                (src, ahead, dst_z.at[0]),
                (src, behind, dst_z.at[1]),
            )
        ):
            copies.append(
                pltpu.make_async_remote_copy(
                    src_ref=piece,
                    dst_ref=place,
                    send_sem=side_send.at[which, side],
                    recv_sem=side_recv.at[which, side],
                    device_id=target,
                    device_id_type=MESH,
                )
            )
        pending.extend(copies)
        return copies

    def rows_send(which, row):
        rows[which, pln] = row
        for off in range(1, npln):
            copy = pltpu.make_async_remote_copy(
                src_ref=rows.at[which, pln],
                dst_ref=rows.at[which, pln],
                send_sem=row_send.at[which],
                recv_sem=row_recv.at[which],
                device_id=(sub, (pln + off) % npln),
                device_id_type=MESH,
            )
            copy.start()

    def rows_wait(which):
        both = rows.at[which, pl.ds(0, npln - 1)]
        pltpu.make_async_copy(both, both, row_recv.at[which]).wait()
        result = rows[which, 0]
        for i in range(1, npln):
            result = result + rows[which, i]
        return result

    def sums_send(which, stage, row):
        count, me, peers = groups[stage]
        sums[which, stage, me] = row
        for peer in peers:
            copy = pltpu.make_async_remote_copy(
                src_ref=sums.at[which, stage, me],
                dst_ref=sums.at[which, stage, me],
                send_sem=sum_send.at[which, stage],
                recv_sem=sum_recv.at[which, stage],
                device_id=peer,
                device_id_type=MESH,
            )
            copy.start()

    def sums_wait(which, stage):
        count, _, _ = groups[stage]
        both = sums.at[which, stage, pl.ds(0, count - 1)]
        pltpu.make_async_copy(both, both, sum_recv.at[which, stage]).wait()
        result = sums[which, stage, 0]
        for i in range(1, count):
            result = result + sums[which, stage, i]
        return result

    lane = lax.broadcasted_iota(jnp.int32, (1, depth), 1)

    def whole(value):
        if value.ndim == 3:
            value = jnp.sum(value.reshape(-1, 8, value.shape[-1]), axis=0)
        return jnp.sum(jnp.sum(value, axis=0, keepdims=True), axis=1, keepdims=True)

    def packet(*values):
        row = jnp.zeros((1, depth), jnp.float32)
        for i, value in enumerate(values):
            row = jnp.where(lane == i, value, row)
        return row

    def entry(row, i):
        return jnp.sum(jnp.where(lane == i, row, 0.0), axis=1, keepdims=True)

    def project_some(value, start, stop):
        @pl.loop(start // STEP, stop // STEP)
        def _(block):
            for inner in range(STEP):
                k = block * STEP + inner
                product = z[k].astype(jnp.float32) * value
                slim = jnp.sum(product.reshape(-1, 8, depth), axis=0)
                part[pl.ds(k, 1), :] = jnp.sum(slim, axis=0, keepdims=True)

    def project_row():
        ones = jnp.ones((8, depth), jnp.float32)
        gathered = lax.dot_general(
            ones, part[...], (((1,), (1,)), ((), ())), precision=PRECISE,
            preferred_element_type=jnp.float32,
        )
        row = gathered[:1]
        return jnp.concatenate([row, jnp.zeros((1, depth - modes), jnp.float32)], axis=1)

    def spread_row(row):
        here = lax.broadcasted_iota(jnp.int32, (modes, depth), 0)
        there = lax.broadcasted_iota(jnp.int32, (modes, depth), 1)
        picked = jnp.where(here == there, jnp.broadcast_to(row, (modes, depth)), 0.0)
        spread[...] = jnp.broadcast_to(jnp.sum(picked, axis=1, keepdims=True), (modes, depth))

    def expand_plane(plane):
        def some(block, acc):
            for inner in range(STEP):
                k = block * STEP + inner
                scale = jnp.broadcast_to(spread[pl.ds(k, 1), :], (height, depth))
                acc = acc + z[k, plane].astype(jnp.float32) * scale
            return acc

        return lax.fori_loop(0, modes // STEP, some, jnp.zeros((height, depth), jnp.float32))

    y_index = lax.broadcasted_iota(jnp.int32, (planes, height, depth), 1)
    z_index = lax.broadcasted_iota(jnp.int32, (planes, height, depth), 2)

    def along_z(value, before, after):
        low = jnp.where(z_index == 0, pltpu.roll(before, 1, 2), pltpu.roll(value, 1, 2))
        high = jnp.where(
            z_index == depth - 1,
            pltpu.roll(after, depth - 1, 2),
            pltpu.roll(value, depth - 1, 2),
        )
        return low, high

    def stencil(which):
        value = field[which]
        zero = jnp.zeros_like(value)
        x_low = jnp.where(first_pln, 0.0, field_x[which, 0])
        x_high = jnp.where(last_pln, 0.0, field_x[which, 1])
        x_below = jnp.concatenate([x_low[None], value[:-1]], axis=0)
        x_above = jnp.concatenate([value[1:], x_high[None]], axis=0)
        y_below = jnp.where(y_index == 0, zero, pltpu.roll(value, 1, 1))
        y_above = jnp.where(y_index == height - 1, zero, pltpu.roll(value, height - 1, 1))
        z_below, z_above = along_z(value, field_z[which, 0], field_z[which, 1])
        return (
            wts[0] * (value - x_below)
            + wts[1] * (value - x_above)
            + wts[2] * (value - y_below)
            + wts[3] * (value - y_above)
            + wts[4] * (value - z_below)
            + wts[5] * (value - z_above)
        )

    small[0].wait()
    label_copies = side_copies(0, lab, lab_x, lab_z)
    for copy in label_copies:
        copy.start()

    small[1].wait()
    for i in range(ZCHUNKS):
        big[i].wait()
        project_some(res[...], i * per, (i + 1) * per)
    rows_send(0, project_row())

    def density(labels):
        value = jnp.full(labels.shape, levels[0], jnp.float32)
        for i in range(1, levels.shape[0]):
            value = jnp.where(labels == i, levels[i], value)
        return value

    for copy in label_copies:
        copy.wait_recv()
    coef = density(lab[...])
    low = jnp.where(first_pln, coef[0], density(lab_x[0]))
    high = jnp.where(last_pln, coef[planes - 1], density(lab_x[1]))
    wts[0] = harmonic(coef, jnp.concatenate([low[None], coef[:-1]], axis=0))
    wts[1] = harmonic(coef, jnp.concatenate([coef[1:], high[None]], axis=0))
    wts[2] = harmonic(coef, jnp.where(y_index == 0, coef, pltpu.roll(coef, 1, 1)))
    wts[3] = harmonic(
        coef, jnp.where(y_index == height - 1, coef, pltpu.roll(coef, height - 1, 1))
    )
    z_low, z_high = along_z(coef, density(lab_z[0]), density(lab_z[1]))
    wts[4] = harmonic(coef, z_low)
    wts[5] = harmonic(coef, z_high)

    def expand(which):
        copies = side_copies(which + 1, field.at[which], field_x.at[which], field_z.at[which])
        for plane in range(planes):
            field[which, plane] = expand_plane(plane)
            if plane == 0:
                copies[1].start()
        copies[0].start()
        copies[2].start()
        copies[3].start()
        return copies

    share = 1.0 / npln
    rhs = rows_wait(0)
    spread_row(rhs)
    copies = expand(0)
    norm_part = jnp.sum(rhs * rhs, axis=1, keepdims=True) * share
    for copy in copies:
        copy.wait_recv()
    image = stencil(0)
    sums_send(0, 0, packet(norm_part, whole(field[0] * image)))
    project_some(image, 0, modes)
    rows_send(1, project_row())
    sums_send(0, 1, sums_wait(0, 0))

    image_row = rows_wait(1)
    spread_row(image_row)
    copies = expand(1)
    sums_send(0, 2, sums_wait(0, 1))
    for copy in copies:
        copy.wait_recv()
    image_next = stencil(1)
    firsts = sums_wait(0, 2)
    norm = entry(firsts, 0)
    curve = entry(firsts, 1)
    alpha = norm / curve
    remain = rhs - alpha * image_row
    remain_field = field[0] - alpha[:, :, None] * field[1]
    remain_image = image - alpha[:, :, None] * image_next
    sums_send(
        1,
        0,
        packet(
            jnp.sum(remain * remain, axis=1, keepdims=True) * share,
            jnp.sum(remain * image_row, axis=1, keepdims=True) * share,
            whole(remain_field * remain_image),
        ),
    )
    sums_send(1, 1, sums_wait(1, 0))
    sums_send(1, 2, sums_wait(1, 1))
    seconds = sums_wait(1, 2)
    norm_next = entry(seconds, 0)
    beta = norm_next / norm
    curve_next = entry(seconds, 2) + 2.0 * beta * entry(seconds, 1) + beta * beta * curve
    alpha_next = norm_next / curve_next
    solution_row = alpha * rhs + alpha_next * (remain + beta * rhs)
    sol_ref[...] = solution_row[:, :modes]
    first_part = (alpha + alpha_next * beta)[:, :, None]
    defl_ref[...] = res[...] - first_part * image - alpha_next[:, :, None] * remain_image

    for copy in pending:
        copy.wait_send()
    for which in range(2):
        both = rows.at[which, pl.ds(0, npln - 1)]
        pltpu.make_async_copy(both, both, row_send.at[which]).wait()
        for stage, (count, _, _) in enumerate(groups):
            both = sums.at[which, stage, pl.ds(0, count - 1)]
            pltpu.make_async_copy(both, both, sum_send.at[which, stage]).wait()


def body(sides, labels, levels, zvec, resid):
    modes = zvec.shape[0]
    block = resid.shape
    ny, nz, npln = sides
    widest = max(npln * 2, nz, ny)
    lanes = block[-1]
    anywhere = pl.BlockSpec(memory_space=pltpu.HBM)
    vmem = pl.BlockSpec(memory_space=pltpu.VMEM)
    dma = pltpu.SemaphoreType.DMA
    return pl.pallas_call(
        functools.partial(kernel, sides),
        out_shape=(
            jax.ShapeDtypeStruct((1, modes), jnp.float32),
            jax.ShapeDtypeStruct(block, jnp.float32),
        ),
        in_specs=[pl.BlockSpec(memory_space=pltpu.SMEM), anywhere, anywhere, anywhere],
        out_specs=(vmem, vmem),
        scratch_shapes=[
            pltpu.VMEM(zvec.shape, zvec.dtype),
            pltpu.VMEM(block, labels.dtype),
            pltpu.VMEM(block, jnp.float32),
            pltpu.VMEM((2,) + block[1:], labels.dtype),
            pltpu.VMEM((2,) + block, labels.dtype),
            pltpu.VMEM((2,) + block, jnp.float32),
            pltpu.VMEM((2, 2) + block[1:], jnp.float32),
            pltpu.VMEM((2, 2) + block, jnp.float32),
            pltpu.VMEM((modes, lanes), jnp.float32),
            pltpu.VMEM((modes, lanes), jnp.float32),
            pltpu.VMEM((2, npln, 1, lanes), jnp.float32),
            pltpu.VMEM((2, 3, widest, 1, lanes), jnp.float32),
            pltpu.VMEM((6,) + block, jnp.float32),
            dma((2 + ZCHUNKS,)),
            dma((3, 4)),
            dma((3, 4)),
            dma((2,)),
            dma((2,)),
            dma((2, 3)),
            dma((2, 3)),
        ],
        compiler_params=pltpu.CompilerParams(
            collective_id=0, has_side_effects=True, vmem_limit_bytes=63 << 20
        ),
        name="deflated_coarse",
    )(levels, labels, zvec, resid)


def solution(mesh):
    chips = mesh.shape["sub"] // 2
    side = math.isqrt(chips)
    sides = (chips // side, side, mesh.shape["pln"])
    in_specs = (P("pln", None, "sub"), P(), P(None, "pln", None, "sub"), P("pln", None, "sub"))
    out_specs = (P("sub", None), P("pln", None, "sub"))
    return jax.shard_map(
        functools.partial(body, sides), mesh=mesh, in_specs=in_specs, out_specs=out_specs,
        check_vma=False,
    )
```

```python
import functools
import math

import jax
import jax.numpy as jnp
from jax import lax
from jax.experimental import pallas as pl
from jax.experimental.pallas import tpu as pltpu
from jax.sharding import PartitionSpec as P

MESH = pl.DeviceIdType.MESH
PRECISE = lax.Precision.HIGHEST
ZCHUNKS = 4
STEP = 4
SLOT = 16
RR, DQ, UU, UQ, QQ, S1, S2, S3 = range(8)


def harmonic(left_value, right_value):
    return 2.0 * left_value * right_value / (left_value + right_value)


def kernel(
    sides,
    levels,
    labels_hbm,
    z_hbm,
    resid_hbm,
    sol_ref,
    defl_ref,
    z,
    lab,
    res,
    lab_send,
    lab_x,
    field,
    field_x,
    edge_send,
    edge,
    edge_modes,
    spread,
    part,
    rows,
    near,
    wide,
    wts,
    load_sem,
    side_send,
    side_recv,
    row_send,
    row_recv,
    sum_send,
    sum_recv,
):
    ny, nz, npln = sides
    nsub = ny * nz * 2
    modes, planes, height, depth = z.shape
    tiles = planes * height // 8
    per_plane = height // 8
    sub = lax.axis_index("sub")
    pln = lax.axis_index("pln")
    core = sub % 2
    zc = (sub // 2) % nz
    yc = sub // (2 * nz)
    first_pln = pln == 0
    last_pln = pln == npln - 1

    per = modes // ZCHUNKS
    res_copy = pltpu.make_async_copy(resid_hbm, res, load_sem.at[0])
    lab_copy = pltpu.make_async_copy(labels_hbm, lab, load_sem.at[1])
    big = [
        pltpu.make_async_copy(
            z_hbm.at[pl.ds(i * per, per)], z.at[pl.ds(i * per, per)], load_sem.at[2 + i]
        )
        for i in range(ZCHUNKS)
    ]
    res_copy.start()
    for copy in big:
        copy.start()
    lab_copy.start()

    halves = npln // 2
    half = pln // 2
    near_count, near_me = 2 * nz, (pln % 2) * nz + zc
    wide_count, wide_me = halves * ny * 2, (half * ny + yc) * 2 + core
    near_peers = []
    for off in range(1, near_count):
        other = (near_me + off) % near_count
        near_peers.append(
            ((yc * nz + other % nz) * 2 + core, pln - pln % 2 + other // nz)
        )
    wide_peers = []
    for off in range(1, wide_count):
        other = (wide_me + off) % wide_count
        apart = other // (2 * ny) - half
        wide_peers.append(
            (
                (((other // 2) % ny) * nz + zc) * 2 + other % 2,
                pln + apart * apart * (npln - 1 - 2 * pln),
            )
        )
    ahead = ((sub + 1) % nsub, pln)
    behind = ((sub + nsub - 1) % nsub, pln)
    right = (sub, (pln + 1) % npln)
    left = (sub, (pln + npln - 1) % npln)
    across = [(sub, (pln + off) % npln) for off in range(1, npln)]
    others = [((sub + 2 * core + nsub - 1) % nsub, pln)] + near_peers + wide_peers
    if halves > 1:
        others.append((sub, (pln + 2) % npln))

    barrier = pltpu.get_barrier_semaphore()
    for peer in others:
        pl.semaphore_signal(barrier, inc=1, device_id=peer, device_id_type=MESH)

    def remote(src, dst, send, recv, target):
        return pltpu.make_async_remote_copy(
            src_ref=src, dst_ref=dst, send_sem=send, recv_sem=recv,
            device_id=target, device_id_type=MESH,
        )

    pending = []

    def plane_copies(which, src, dst):
        copies = [
            remote(src.at[planes - 1], dst.at[0], side_send.at[which, 0],
                   side_recv.at[which, 0], right),
            remote(src.at[0], dst.at[1], side_send.at[which, 1], side_recv.at[which, 1], left),
        ]
        pending.extend(copies)
        return copies

    def edge_copies(which):
        copies = [
            remote(edge_send.at[which], edge.at[which, i], side_send.at[which, 2 + i],
                   side_recv.at[which, 2 + i], target)
            for i, target in enumerate((ahead, behind))
        ]
        pending.extend(copies)
        return copies

    def rows_send(which, row):
        rows[which, pln] = row
        mine = rows.at[which, pln]
        for peer in across:
            remote(mine, mine, row_send.at[which], row_recv.at[which], peer).start()

    def rows_wait(which):
        both = rows.at[which, pl.ds(0, npln - 1)]
        pltpu.make_async_copy(both, both, row_recv.at[which]).wait()
        result = rows[which, 0]
        for i in range(1, npln):
            result = result + rows[which, i]
        return result

    lane = lax.broadcasted_iota(jnp.int32, (1, depth), 1)
    lane8 = lax.broadcasted_iota(jnp.int32, (8, depth), 1)

    def across_lanes(value):
        return jnp.sum(value, axis=1, keepdims=True)

    def whole(value):
        slim = jnp.sum(value.reshape(-1, 8, depth), axis=0)
        return across_lanes(jnp.sum(slim, axis=0, keepdims=True))

    def tile_of(value, j):
        row = (j % per_plane) * 8
        return value[j // per_plane, row:row + 8, :]

    def pack_edges(value):
        packed = jnp.zeros((8, depth), jnp.float32)
        for j in range(tiles):
            rolled = pltpu.roll(tile_of(value, j), 2 * j + 1, 1)
            packed = jnp.where(lane8 // 2 == j, rolled, packed)
        return packed

    def unpack_behind(packed):
        pieces = [pltpu.roll(packed, (depth - 2 * j) % depth, 1) for j in range(tiles)]
        return jnp.concatenate(pieces, axis=0).reshape(planes, height, depth)

    def unpack_ahead(packed):
        pieces = [pltpu.roll(packed, depth - 2 - 2 * j, 1) for j in range(tiles)]
        return jnp.concatenate(pieces, axis=0).reshape(planes, height, depth)

    def project_some(value, start, stop):
        @pl.loop(start // STEP, stop // STEP)
        def _(block):
            for inner in range(STEP):
                k = block * STEP + inner
                product = z[k].astype(jnp.float32) * value
                slim = jnp.sum(product.reshape(-1, 8, depth), axis=0)
                part[pl.ds(k, 1), :] = jnp.sum(slim, axis=0, keepdims=True)

    def project_row():
        ones = jnp.ones((8, depth), jnp.float32)
        gathered = lax.dot_general(
            ones, part[...], (((1,), (1,)), ((), ())), precision=PRECISE,
            preferred_element_type=jnp.float32,
        )
        row = gathered[:1]
        return jnp.concatenate([row, jnp.zeros((1, depth - modes), jnp.float32)], axis=1)

    def spread_row(row):
        here = lax.broadcasted_iota(jnp.int32, (modes, depth), 0)
        there = lax.broadcasted_iota(jnp.int32, (modes, depth), 1)
        picked = jnp.where(here == there, jnp.broadcast_to(row, (modes, depth)), 0.0)
        spread[...] = jnp.broadcast_to(across_lanes(picked), (modes, depth))

    def expand_edges():
        def some(block, acc):
            for inner in range(8):
                k = block * 8 + inner
                acc = acc + edge_modes[k] * jnp.broadcast_to(spread[pl.ds(k, 1), :], (8, depth))
            return acc

        return lax.fori_loop(0, modes // 8, some, jnp.zeros((8, depth), jnp.float32))

    def expand_plane(plane):
        def some(block, acc):
            for inner in range(STEP):
                k = block * STEP + inner
                scale = jnp.broadcast_to(spread[pl.ds(k, 1), :], (height, depth))
                acc = acc + z[k, plane].astype(jnp.float32) * scale
            return acc

        return lax.fori_loop(0, modes // STEP, some, jnp.zeros((height, depth), jnp.float32))

    def expand(which, row):
        spread_row(row)
        edge_send[which + 1] = expand_edges()
        edges = edge_copies(which + 1)
        for copy in edges:
            copy.start()
        sides_x = plane_copies(which + 1, field.at[which], field_x.at[which])
        field[which, 0] = expand_plane(0)
        sides_x[1].start()
        for plane in range(1, planes):
            field[which, plane] = expand_plane(plane)
        sides_x[0].start()
        return edges + sides_x

    y_index = lax.broadcasted_iota(jnp.int32, (planes, height, depth), 1)
    z_index = lax.broadcasted_iota(jnp.int32, (planes, height, depth), 2)

    def along_z(value, before, after):
        low = jnp.where(z_index == 0, unpack_behind(before), pltpu.roll(value, 1, 2))
        high = jnp.where(
            z_index == depth - 1, unpack_ahead(after), pltpu.roll(value, depth - 1, 2)
        )
        return low, high

    def stencil(which):
        value = field[which]
        zero = jnp.zeros_like(value)
        x_low = jnp.where(first_pln, 0.0, field_x[which, 0])
        x_high = jnp.where(last_pln, 0.0, field_x[which, 1])
        x_below = jnp.concatenate([x_low[None], value[:-1]], axis=0)
        x_above = jnp.concatenate([value[1:], x_high[None]], axis=0)
        y_below = jnp.where(y_index == 0, zero, pltpu.roll(value, 1, 1))
        y_above = jnp.where(y_index == height - 1, zero, pltpu.roll(value, height - 1, 1))
        z_below, z_above = along_z(value, edge[which + 1, 0], edge[which + 1, 1])
        return (
            wts[0] * (value - x_below)
            + wts[1] * (value - x_above)
            + wts[2] * (value - y_below)
            + wts[3] * (value - y_above)
            + wts[4] * (value - z_below)
            + wts[5] * (value - z_above)
        )

    res_copy.wait()
    for i in range(ZCHUNKS):
        big[i].wait()
        project_some(res[...], i * per, (i + 1) * per)
    rhs_part = project_row()
    pl.semaphore_wait(barrier, len(others))
    rows_send(0, rhs_part)

    lab_copy.wait()
    narrow = lab[...].astype(jnp.float32)
    lab_send[...] = narrow.astype(jnp.bfloat16)
    edge_send[0] = pack_edges(narrow)
    label_copies = edge_copies(0) + plane_copies(0, lab_send, lab_x)
    for copy in label_copies:
        copy.start()

    @pl.loop(0, modes // 2)
    def _(block):
        for inner in range(2):
            k = block * 2 + inner
            edge_modes[k] = pack_edges(z[k].astype(jnp.float32))

    def density(labels):
        value = jnp.full(labels.shape, levels[0], jnp.float32)
        for i in range(1, levels.shape[0]):
            value = jnp.where(labels == float(i), levels[i], value)
        return value

    for copy in label_copies:
        copy.wait_recv()
    coef = density(lab[...].astype(jnp.float32))
    low = jnp.where(first_pln, coef[0], density(lab_x[0].astype(jnp.float32)))
    high = jnp.where(last_pln, coef[planes - 1], density(lab_x[1].astype(jnp.float32)))
    wts[0] = harmonic(coef, jnp.concatenate([low[None], coef[:-1]], axis=0))
    wts[1] = harmonic(coef, jnp.concatenate([coef[1:], high[None]], axis=0))
    wts[2] = harmonic(coef, jnp.where(y_index == 0, coef, pltpu.roll(coef, 1, 1)))
    wts[3] = harmonic(
        coef, jnp.where(y_index == height - 1, coef, pltpu.roll(coef, height - 1, 1))
    )
    z_low, z_high = along_z(coef, density(edge[0, 0]), density(edge[0, 1]))
    wts[4] = harmonic(coef, z_low)
    wts[5] = harmonic(coef, z_high)

    rhs = rows_wait(0)
    for copy in expand(0, rhs):
        copy.wait_recv()
    image = stencil(0)
    project_some(image, 0, modes)
    rows_send(1, project_row())

    image_row = rows_wait(1)
    copies = expand(1, image_row)
    dq = across_lanes(rhs * image_row)
    qq = across_lanes(image_row * image_row)
    guess = jnp.where(qq > 0.0, dq / jnp.where(qq > 0.0, qq, 1.0), 0.0)
    rest = rhs - guess * image_row
    shared = {
        RR: across_lanes(rhs * rhs),
        DQ: dq,
        UU: across_lanes(rest * rest),
        UQ: across_lanes(rest * image_row),
        QQ: qq,
    }
    spot = lane - SLOT * zc
    packet = jnp.zeros((1, depth), jnp.float32)
    for i, value in shared.items():
        packet = jnp.where(spot == i, jnp.where(first_pln, value, 0.0), packet)
    guesses = jnp.where(
        jnp.logical_and(spot >= 0, spot < SLOT), jnp.where(first_pln, guess, 0.0), 0.0
    )
    for copy in copies:
        copy.wait_recv()
    image_next = stencil(1)
    guess3 = guess[:, :, None]
    rest_field = field[0] - guess3 * field[1]
    rest_image = image - guess3 * image_next
    local = {
        S1: whole(rest_field * rest_image),
        S2: whole(rest_field * image_next + field[1] * rest_image),
        S3: whole(field[1] * image_next),
    }
    for i, value in local.items():
        packet = jnp.where(spot == i, value, packet)

    near[near_me] = jnp.concatenate([packet, guesses], axis=0)
    mine = near.at[near_me]
    for peer in near_peers:
        remote(mine, mine, sum_send.at[0], sum_recv.at[0], peer).start()
    both = near.at[pl.ds(0, near_count - 1)]
    pltpu.make_async_copy(both, both, sum_recv.at[0]).wait()
    wide[wide_me] = jnp.sum(near[...], axis=0)
    mine = wide.at[wide_me]
    for peer in wide_peers:
        remote(mine, mine, sum_send.at[1], sum_recv.at[1], peer).start()
    both = wide.at[pl.ds(0, wide_count - 1)]
    pltpu.make_async_copy(both, both, sum_recv.at[1]).wait()
    count = wide_count // halves
    pairs = []
    for i in range(count):
        pair = wide[i]
        for j in range(1, halves):
            pair = pair + wide[j * count + i]
        pairs.append(pair)
    table = jnp.concatenate(pairs, axis=0)
    shape = table.shape
    upper = lax.broadcasted_iota(jnp.int32, shape, 0) % 2 == 0
    kind = jnp.where(upper, lax.broadcasted_iota(jnp.int32, shape, 1) % SLOT, SLOT)
    step_guess = pltpu.roll(table, shape[0] - 1, 0)

    def total(value):
        return across_lanes(jnp.sum(value, axis=0, keepdims=True))

    norm = total(jnp.where(kind == RR, table, 0.0))
    curve = total(jnp.where(kind == DQ, table, 0.0))
    alpha = norm / curve
    delta = alpha - step_guess
    squared = delta * delta * table
    norm_next = total(
        jnp.where(kind == UU, table, 0.0)
        + jnp.where(kind == UQ, -2.0 * delta * table, 0.0)
        + jnp.where(kind == QQ, squared, 0.0)
    )
    curve_rest = total(
        jnp.where(kind == S1, table, 0.0)
        + jnp.where(kind == S2, -delta * table, 0.0)
        + jnp.where(kind == S3, squared, 0.0)
    )
    mixed = total(
        jnp.where(kind == UQ, table, 0.0) + jnp.where(kind == QQ, -delta * table, 0.0)
    )
    beta = norm_next / norm
    curve_next = curve_rest + 2.0 * beta * mixed + beta * beta * curve
    alpha_next = norm_next / curve_next
    first_part = alpha + alpha_next * (1.0 + beta)
    second_part = alpha_next * alpha
    solution_row = first_part * rhs - second_part * image_row
    sol_ref[...] = solution_row[:, :modes]
    defl_ref[...] = (
        res[...] - first_part[:, :, None] * image + second_part[:, :, None] * image_next
    )

    for copy in pending:
        copy.wait_send()
    for which in range(2):
        both = rows.at[which, pl.ds(0, npln - 1)]
        pltpu.make_async_copy(both, both, row_send.at[which]).wait()
    both = near.at[pl.ds(0, near_count - 1)]
    pltpu.make_async_copy(both, both, sum_send.at[0]).wait()
    both = wide.at[pl.ds(0, wide_count - 1)]
    pltpu.make_async_copy(both, both, sum_send.at[1]).wait()


def body(sides, labels, levels, zvec, resid):
    modes = zvec.shape[0]
    block = resid.shape
    ny, nz, npln = sides
    lanes = block[-1]
    in_hbm = pl.BlockSpec(memory_space=pltpu.HBM)
    vmem = pl.BlockSpec(memory_space=pltpu.VMEM)
    dma = pltpu.SemaphoreType.DMA
    wide = jnp.float32
    return pl.pallas_call(
        functools.partial(kernel, sides),
        out_shape=(
            jax.ShapeDtypeStruct((1, modes), wide),
            jax.ShapeDtypeStruct(block, wide),
        ),
        in_specs=[pl.BlockSpec(memory_space=pltpu.SMEM), in_hbm, in_hbm, in_hbm],
        out_specs=(vmem, vmem),
        scratch_shapes=[
            pltpu.VMEM(zvec.shape, zvec.dtype),
            pltpu.VMEM(block, labels.dtype),
            pltpu.VMEM(block, wide),
            pltpu.VMEM(block, jnp.bfloat16),
            pltpu.VMEM((2,) + block[1:], jnp.bfloat16),
            pltpu.VMEM((2,) + block, wide),
            pltpu.VMEM((2, 2) + block[1:], wide),
            pltpu.VMEM((3, 8, lanes), wide),
            pltpu.VMEM((3, 2, 8, lanes), wide),
            pltpu.VMEM((modes, 8, lanes), wide),
            pltpu.VMEM((modes, lanes), wide),
            pltpu.VMEM((modes, lanes), wide),
            pltpu.VMEM((2, npln, 1, lanes), wide),
            pltpu.VMEM((2 * nz, 2, lanes), wide),
            pltpu.VMEM((npln * ny, 2, lanes), wide),
            pltpu.VMEM((6,) + block, wide),
            dma((2 + ZCHUNKS,)),
            dma((3, 4)),
            dma((3, 4)),
            dma((2,)),
            dma((2,)),
            dma((2,)),
            dma((2,)),
        ],
        compiler_params=pltpu.CompilerParams(
            collective_id=0, has_side_effects=True, vmem_limit_bytes=63 << 20
        ),
        name="deflated_coarse",
    )(levels, labels, zvec, resid)


def solution(mesh):
    chips = mesh.shape["sub"] // 2
    side = math.isqrt(chips)
    sides = (chips // side, side, mesh.shape["pln"])
    in_specs = (P("pln", None, "sub"), P(), P(None, "pln", None, "sub"), P("pln", None, "sub"))
    out_specs = (P("sub", None), P("pln", None, "sub"))
    return jax.shard_map(
        functools.partial(body, sides), mesh=mesh, in_specs=in_specs, out_specs=out_specs,
        check_vma=False,
    )
```

```python
import functools
import itertools
import math

import jax
import jax.numpy as jnp
from jax import lax
from jax.experimental import pallas as pl
from jax.experimental.pallas import tpu as pltpu
from jax.sharding import PartitionSpec as P

MESH = pl.DeviceIdType.MESH
PRECISE = lax.Precision.HIGHEST
ZCHUNKS = 4
STEP = 16
SLOT = 16
RR, DQ, UU, UQ, QQ, S1, S2, S3 = range(8)


def harmonic(left_value, right_value):
    return 2.0 * left_value * right_value / (left_value + right_value)


def kernel(
    sides,
    levels_hbm,
    labels_hbm,
    z_hbm,
    resid_hbm,
    sol_ref,
    defl_ref,
    z,
    lab,
    res,
    lab_send,
    lab_x,
    field,
    field_send,
    field_x,
    edge_send,
    edge,
    edge_modes,
    spread,
    part,
    rows,
    near,
    wide,
    wts,
    levels,
    load_sem,
    side_send,
    side_recv,
    row_send,
    row_recv,
    sum_send,
    sum_recv,
):
    ny, nz, npln = sides
    nsub = ny * nz * 2
    modes, planes, height, depth = z.shape
    tiles = planes * height // 8
    per_plane = height // 8
    sub = lax.axis_index("sub")
    pln = lax.axis_index("pln")
    core = lax.rem(sub, 2)
    zc = lax.rem(lax.div(sub, 2), nz)
    yc = lax.div(sub, 2 * nz)
    first_pln = pln == 0
    last_pln = pln == npln - 1

    per = modes // ZCHUNKS
    res_copy = pltpu.make_async_copy(resid_hbm, res, load_sem.at[0])
    lab_copy = pltpu.make_async_copy(labels_hbm, lab, load_sem.at[1])
    big = [
        pltpu.make_async_copy(
            z_hbm.at[pl.ds(i * per, per)], z.at[pl.ds(i * per, per)], load_sem.at[2 + i]
        )
        for i in range(ZCHUNKS)
    ]
    res_copy.start()
    for copy in big:
        copy.start()
    lab_copy.start()
    level_copy = pltpu.make_async_copy(levels_hbm, levels, load_sem.at[2 + ZCHUNKS])
    level_copy.start()

    halves = npln // 2
    odd, half = lax.rem(pln, 2), lax.div(pln, 2)
    near_count, near_me = 2 * nz, odd * nz + zc
    wide_count, wide_me = halves * ny * 2, (half * ny + yc) * 2 + core

    def offsets(*sizes):
        def hops(offset):
            return sum(min(step, size - step) for step, size in zip(offset, sizes))

        every = list(itertools.product(*(range(size) for size in sizes)))
        return sorted(every[1:], key=hops, reverse=True)

    near_peers = [
        (sub - 2 * zc + 2 * lax.rem(zc + step, nz), pln + flip * (1 - 2 * odd))
        for flip, step in offsets(2, nz)
    ]
    wide_peers = [
        (
            (lax.rem(yc + step, ny) * nz + zc) * 2 + (1 - core if other else core),
            npln - 1 - pln if flip else pln,
        )
        for flip, step, other in offsets(halves, ny, 2)
    ]
    ahead = (lax.rem(sub + 1, nsub), pln)
    behind = (lax.rem(sub + nsub - 1, nsub), pln)
    right = (sub, lax.rem(pln + 1, npln))
    left = (sub, lax.rem(pln + npln - 1, npln))
    across = [(sub, lax.rem(pln + off, npln)) for off in (2, 1, 3) if off < npln]
    others = [(lax.rem(sub + 2 * core + nsub - 1, nsub), pln)] + near_peers + wide_peers
    if halves > 1:
        others.append((sub, lax.rem(pln + 2, npln)))

    barrier = pltpu.get_barrier_semaphore()
    for peer in others:
        pl.semaphore_signal(barrier, inc=1, device_id=peer, device_id_type=MESH)

    def remote(src, dst, send, recv, target):
        return pltpu.make_async_remote_copy(
            src_ref=src, dst_ref=dst, send_sem=send, recv_sem=recv,
            device_id=target, device_id_type=MESH,
        )

    pending = []

    def plane_copies(which, src, dst):
        copies = [
            remote(src.at[planes - 1], dst.at[0], side_send.at[which, 0],
                   side_recv.at[which, 0], right),
            remote(src.at[0], dst.at[1], side_send.at[which, 1], side_recv.at[which, 1], left),
        ]
        pending.extend(copies)
        return copies

    def edge_copies(which):
        copies = [
            remote(edge_send.at[which], edge.at[which, i], side_send.at[which, 2 + i],
                   side_recv.at[which, 2 + i], target)
            for i, target in enumerate((ahead, behind))
        ]
        pending.extend(copies)
        return copies

    def rows_send(which, row):
        rows[which, pln] = row
        mine = rows.at[which, pln]
        for peer in across:
            remote(mine, mine, row_send.at[which], row_recv.at[which], peer).start()

    def rows_wait(which):
        both = rows.at[which, pl.ds(0, npln - 1)]
        pltpu.make_async_copy(both, both, row_recv.at[which]).wait()
        result = rows[which, 0]
        for i in range(1, npln):
            result = result + rows[which, i]
        return result

    lane = lax.broadcasted_iota(jnp.int32, (1, depth), 1)
    lane8 = lax.broadcasted_iota(jnp.int32, (8, depth), 1)

    def across_lanes(value):
        return jnp.sum(value, axis=1, keepdims=True)

    def whole(value):
        slim = jnp.sum(value.reshape(-1, 8, depth), axis=0)
        return across_lanes(jnp.sum(slim, axis=0, keepdims=True))

    def tile_of(value, j):
        row = (j % per_plane) * 8
        return value[j // per_plane, row:row + 8, :]

    def pack_edges(value):
        packed = jnp.zeros((8, depth), jnp.float32)
        for j in range(tiles):
            rolled = pltpu.roll(tile_of(value, j), 2 * j + 1, 1)
            packed = jnp.where(lane8 // 2 == j, rolled, packed)
        return packed

    def unpack_behind(packed):
        pieces = [pltpu.roll(packed, (depth - 2 * j) % depth, 1) for j in range(tiles)]
        return jnp.concatenate(pieces, axis=0).reshape(planes, height, depth)

    def unpack_ahead(packed):
        pieces = [pltpu.roll(packed, depth - 2 - 2 * j, 1) for j in range(tiles)]
        return jnp.concatenate(pieces, axis=0).reshape(planes, height, depth)

    def project_some(value, start, stop):
        @pl.loop(start // STEP, stop // STEP)
        def _(block):
            for inner in range(STEP):
                k = block * STEP + inner
                product = z[k].astype(jnp.float32) * value
                slim = jnp.sum(product.reshape(-1, 8, depth), axis=0)
                part[pl.ds(k, 1), :] = jnp.sum(slim, axis=0, keepdims=True)

    def project_row():
        ones = jnp.ones((8, depth), jnp.float32)
        gathered = lax.dot_general(
            ones, part[...], (((1,), (1,)), ((), ())), precision=PRECISE,
            preferred_element_type=jnp.float32,
        )
        row = gathered[:1]
        return jnp.concatenate([row, jnp.zeros((1, depth - modes), jnp.float32)], axis=1)

    def spread_row(row):
        here = lax.broadcasted_iota(jnp.int32, (modes, depth), 0)
        there = lax.broadcasted_iota(jnp.int32, (modes, depth), 1)
        picked = jnp.where(here == there, jnp.broadcast_to(row, (modes, depth)), 0.0)
        spread[...] = jnp.broadcast_to(across_lanes(picked), (modes, depth))

    def expand_edges():
        def some(block, acc):
            for inner in range(8):
                k = block * 8 + inner
                acc = acc + edge_modes[k] * jnp.broadcast_to(spread[pl.ds(k, 1), :], (8, depth))
            return acc

        return lax.fori_loop(0, modes // 8, some, jnp.zeros((8, depth), jnp.float32))

    def expand_plane(plane):
        def some(block, acc):
            for inner in range(STEP):
                k = block * STEP + inner
                scale = jnp.broadcast_to(spread[pl.ds(k, 1), :], (height, depth))
                acc = acc + z[k, plane].astype(jnp.float32) * scale
            return acc

        return lax.fori_loop(0, modes // STEP, some, jnp.zeros((height, depth), jnp.float32))

    def expand(which, row):
        spread_row(row)
        edge_send[which + 1] = expand_edges()
        edges = edge_copies(which + 1)
        for copy in edges:
            copy.start()
        sides_x = plane_copies(which + 1, field_send.at[which], field_x.at[which])
        for plane in range(planes):
            value = expand_plane(plane)
            field[which, plane] = value
            field_send[which, plane] = value.astype(jnp.bfloat16)
            if plane == 0:
                sides_x[1].start()
        sides_x[0].start()
        return edges + sides_x

    y_index = lax.broadcasted_iota(jnp.int32, (planes, height, depth), 1)
    z_index = lax.broadcasted_iota(jnp.int32, (planes, height, depth), 2)

    def along_z(value, before, after):
        low = jnp.where(z_index == 0, unpack_behind(before), pltpu.roll(value, 1, 2))
        high = jnp.where(
            z_index == depth - 1, unpack_ahead(after), pltpu.roll(value, depth - 1, 2)
        )
        return low, high

    def stencil(which):
        value = field[which]
        zero = jnp.zeros_like(value)
        x_low = jnp.where(first_pln, 0.0, field_x[which, 0].astype(jnp.float32))
        x_high = jnp.where(last_pln, 0.0, field_x[which, 1].astype(jnp.float32))
        x_below = jnp.concatenate([x_low[None], value[:-1]], axis=0)
        x_above = jnp.concatenate([value[1:], x_high[None]], axis=0)
        y_below = jnp.where(y_index == 0, zero, pltpu.roll(value, 1, 1))
        y_above = jnp.where(y_index == height - 1, zero, pltpu.roll(value, height - 1, 1))
        z_below, z_above = along_z(value, edge[which + 1, 0], edge[which + 1, 1])
        return (
            wts[0] * (value - x_below)
            + wts[1] * (value - x_above)
            + wts[2] * (value - y_below)
            + wts[3] * (value - y_above)
            + wts[4] * (value - z_below)
            + wts[5] * (value - z_above)
        )

    res_copy.wait()
    for i in range(ZCHUNKS):
        big[i].wait()
        project_some(res[...], i * per, (i + 1) * per)
    rhs_part = project_row()
    pl.semaphore_wait(barrier, len(others))
    rows_send(0, rhs_part)

    lab_copy.wait()
    level_copy.wait()
    narrow = lab[...].astype(jnp.float32)
    lab_send[...] = narrow.astype(jnp.bfloat16)
    edge_send[0] = pack_edges(narrow)
    label_copies = edge_copies(0) + plane_copies(0, lab_send, lab_x)
    for copy in label_copies:
        copy.start()

    @pl.loop(0, modes // 8)
    def _(block):
        for inner in range(8):
            k = block * 8 + inner
            edge_modes[k] = pack_edges(z[k].astype(jnp.float32))

    def density(labels):
        value = jnp.full(labels.shape, levels[0], jnp.float32)
        for i in range(1, levels.shape[0]):
            value = jnp.where(labels == float(i), levels[i], value)
        return value

    rhs = rows_wait(0)
    copies = expand(0, rhs)
    for copy in label_copies:
        copy.wait_recv()
    coef = density(lab[...].astype(jnp.float32))
    low = jnp.where(first_pln, coef[0], density(lab_x[0].astype(jnp.float32)))
    high = jnp.where(last_pln, coef[planes - 1], density(lab_x[1].astype(jnp.float32)))
    wts[0] = harmonic(coef, jnp.concatenate([low[None], coef[:-1]], axis=0))
    wts[1] = harmonic(coef, jnp.concatenate([coef[1:], high[None]], axis=0))
    wts[2] = harmonic(coef, jnp.where(y_index == 0, coef, pltpu.roll(coef, 1, 1)))
    wts[3] = harmonic(
        coef, jnp.where(y_index == height - 1, coef, pltpu.roll(coef, height - 1, 1))
    )
    z_low, z_high = along_z(coef, density(edge[0, 0]), density(edge[0, 1]))
    wts[4] = harmonic(coef, z_low)
    wts[5] = harmonic(coef, z_high)

    for copy in copies:
        copy.wait_recv()
    image = stencil(0)
    project_some(image, 0, modes)
    rows_send(1, project_row())

    image_row = rows_wait(1)
    copies = expand(1, image_row)
    dq = across_lanes(rhs * image_row)
    qq = across_lanes(image_row * image_row)
    guess = jnp.where(qq > 0.0, dq / jnp.where(qq > 0.0, qq, 1.0), 0.0)
    rest = rhs - guess * image_row
    shared = {
        RR: across_lanes(rhs * rhs),
        DQ: dq,
        UU: across_lanes(rest * rest),
        UQ: across_lanes(rest * image_row),
        QQ: qq,
    }
    spot = lane - SLOT * zc
    packet = jnp.zeros((1, depth), jnp.float32)
    for i, value in shared.items():
        packet = jnp.where(spot == i, jnp.where(first_pln, value, 0.0), packet)
    guesses = jnp.where(
        jnp.logical_and(spot >= 0, spot < SLOT), jnp.where(first_pln, guess, 0.0), 0.0
    )
    for copy in copies:
        copy.wait_recv()
    image_next = stencil(1)
    guess3 = guess[:, :, None]
    rest_field = field[0] - guess3 * field[1]
    rest_image = image - guess3 * image_next
    local = {
        S1: whole(rest_field * rest_image),
        S2: whole(rest_field * image_next + field[1] * rest_image),
        S3: whole(field[1] * image_next),
    }
    for i, value in local.items():
        packet = jnp.where(spot == i, value, packet)

    near[near_me] = jnp.concatenate([packet, guesses], axis=0)
    mine = near.at[near_me]
    for peer in near_peers:
        remote(mine, mine, sum_send.at[0], sum_recv.at[0], peer).start()
    both = near.at[pl.ds(0, near_count - 1)]
    pltpu.make_async_copy(both, both, sum_recv.at[0]).wait()
    wide[wide_me] = jnp.sum(near[...], axis=0)
    mine = wide.at[wide_me]
    for peer in wide_peers:
        remote(mine, mine, sum_send.at[1], sum_recv.at[1], peer).start()
    both = wide.at[pl.ds(0, wide_count - 1)]
    pltpu.make_async_copy(both, both, sum_recv.at[1]).wait()
    count = wide_count // halves
    pairs = []
    for i in range(count):
        pair = wide[i]
        for j in range(1, halves):
            pair = pair + wide[j * count + i]
        pairs.append(pair)
    table = jnp.concatenate(pairs, axis=0)
    shape = table.shape
    upper = lax.broadcasted_iota(jnp.int32, shape, 0) % 2 == 0
    kind = jnp.where(upper, lax.broadcasted_iota(jnp.int32, shape, 1) % SLOT, SLOT)
    step_guess = pltpu.roll(table, shape[0] - 1, 0)

    def total(value):
        return across_lanes(jnp.sum(value, axis=0, keepdims=True))

    norm = total(jnp.where(kind == RR, table, 0.0))
    curve = total(jnp.where(kind == DQ, table, 0.0))
    alpha = norm / curve
    delta = alpha - step_guess
    squared = delta * delta * table
    norm_next = total(
        jnp.where(kind == UU, table, 0.0)
        + jnp.where(kind == UQ, -2.0 * delta * table, 0.0)
        + jnp.where(kind == QQ, squared, 0.0)
    )
    curve_rest = total(
        jnp.where(kind == S1, table, 0.0)
        + jnp.where(kind == S2, -delta * table, 0.0)
        + jnp.where(kind == S3, squared, 0.0)
    )
    mixed = total(
        jnp.where(kind == UQ, table, 0.0) + jnp.where(kind == QQ, -delta * table, 0.0)
    )
    beta = norm_next / norm
    curve_next = curve_rest + 2.0 * beta * mixed + beta * beta * curve
    alpha_next = norm_next / curve_next
    first_part = alpha + alpha_next * (1.0 + beta)
    second_part = alpha_next * alpha
    solution_row = first_part * rhs - second_part * image_row
    sol_ref[...] = solution_row[:, :modes]
    defl_ref[...] = (
        res[...] - first_part[:, :, None] * image + second_part[:, :, None] * image_next
    )

    for copy in pending:
        copy.wait_send()
    for which in range(2):
        both = rows.at[which, pl.ds(0, npln - 1)]
        pltpu.make_async_copy(both, both, row_send.at[which]).wait()
    both = near.at[pl.ds(0, near_count - 1)]
    pltpu.make_async_copy(both, both, sum_send.at[0]).wait()
    both = wide.at[pl.ds(0, wide_count - 1)]
    pltpu.make_async_copy(both, both, sum_send.at[1]).wait()


def finish(row, out, sol_hbm, defl_hbm, sems):
    copies = [
        pltpu.make_async_copy(out, defl_hbm, sems.at[0]),
        pltpu.make_async_copy(row, sol_hbm, sems.at[1]),
    ]
    for copy in copies:
        copy.start()
    for copy in copies:
        copy.wait()


def body(sides, labels, levels, zvec, resid):
    modes = zvec.shape[0]
    block = resid.shape
    ny, nz, npln = sides
    lanes = block[-1]
    in_hbm = pl.BlockSpec(memory_space=pltpu.HBM)
    vmem = pl.BlockSpec(memory_space=pltpu.VMEM)
    dma = pltpu.SemaphoreType.DMA
    wide = jnp.float32
    row, out = pl.pallas_call(
        functools.partial(kernel, sides),
        out_shape=(
            jax.ShapeDtypeStruct((1, modes), wide),
            jax.ShapeDtypeStruct(block, wide),
        ),
        in_specs=[in_hbm] * 4,
        out_specs=(vmem, vmem),
        scratch_shapes=[
            pltpu.VMEM(zvec.shape, zvec.dtype),
            pltpu.VMEM(block, labels.dtype),
            pltpu.VMEM(block, wide),
            pltpu.VMEM(block, jnp.bfloat16),
            pltpu.VMEM((2,) + block[1:], jnp.bfloat16),
            pltpu.VMEM((2,) + block, wide),
            pltpu.VMEM((2,) + block, jnp.bfloat16),
            pltpu.VMEM((2, 2) + block[1:], jnp.bfloat16),
            pltpu.VMEM((3, 8, lanes), wide),
            pltpu.VMEM((3, 2, 8, lanes), wide),
            pltpu.VMEM((modes, 8, lanes), wide),
            pltpu.VMEM((modes, lanes), wide),
            pltpu.VMEM((modes, lanes), wide),
            pltpu.VMEM((2, npln, 1, lanes), wide),
            pltpu.VMEM((2 * nz, 2, lanes), wide),
            pltpu.VMEM((npln * ny, 2, lanes), wide),
            pltpu.VMEM((6,) + block, wide),
            pltpu.SMEM(levels.shape, wide),
            dma((3 + ZCHUNKS,)),
            dma((3, 4)),
            dma((3, 4)),
            dma((2,)),
            dma((2,)),
            dma((2,)),
            dma((2,)),
        ],
        compiler_params=pltpu.CompilerParams(
            collective_id=0, has_side_effects=True, vmem_limit_bytes=24 << 20
        ),
        name="deflated_coarse",
    )(
        *(pltpu.with_memory_space_constraint(a, pltpu.HBM) for a in (levels, labels, zvec, resid))
    )
    return pl.pallas_call(
        finish,
        out_shape=(
            jax.ShapeDtypeStruct((1, modes), wide),
            jax.ShapeDtypeStruct(block, wide),
        ),
        in_specs=[vmem, vmem],
        out_specs=(in_hbm, in_hbm),
        scratch_shapes=[dma((2,))],
        compiler_params=pltpu.CompilerParams(vmem_limit_bytes=2 << 20),
        name="finish",
    )(row, out)


def solution(mesh):
    chips = mesh.shape["sub"] // 2
    side = math.isqrt(chips)
    sides = (chips // side, side, mesh.shape["pln"])
    in_specs = (P("pln", None, "sub"), P(), P(None, "pln", None, "sub"), P("pln", None, "sub"))
    out_specs = (P("sub", None), P("pln", None, "sub"))
    return jax.shard_map(
        functools.partial(body, sides), mesh=mesh, in_specs=in_specs, out_specs=out_specs,
        check_vma=False,
    )
```

```python
import functools
import itertools
import math

import jax
import jax.numpy as jnp
from jax import lax
from jax.experimental import pallas as pl
from jax.experimental.pallas import tpu as pltpu
from jax.sharding import PartitionSpec as P

MESH = pl.DeviceIdType.MESH
PRECISE = lax.Precision.HIGHEST
ZCHUNKS = 4
STEP = 16
SLOT = 16
RR, DQ, UU, UQ, QQ, S1, S2, S3 = range(8)


def harmonic(left_value, right_value):
    return 2.0 * left_value * right_value / (left_value + right_value)


def kernel(
    sides,
    levels_hbm,
    labels_hbm,
    z_hbm,
    resid_hbm,
    sol_ref,
    defl_ref,
    z,
    lab,
    res,
    lab_send,
    lab_x,
    field,
    field_send,
    field_x,
    edge_send,
    edge,
    edge_modes,
    spread,
    part,
    rows,
    near,
    wide,
    wts,
    levels,
    load_sem,
    side_send,
    side_recv,
    row_send,
    row_recv,
    sum_send,
    sum_recv,
    token,
):
    ny, nz, npln = sides
    nsub = ny * nz * 2
    modes, planes, height, depth = z.shape
    tiles = planes * height // 8
    per_plane = height // 8
    sub = lax.axis_index("sub")
    pln = lax.axis_index("pln")
    core = lax.rem(sub, 2)
    zc = lax.rem(lax.div(sub, 2), nz)
    yc = lax.div(sub, 2 * nz)
    first_pln = pln == 0
    last_pln = pln == npln - 1

    per = modes // ZCHUNKS
    res_copy = pltpu.make_async_copy(resid_hbm, res, load_sem.at[0])
    lab_copy = pltpu.make_async_copy(labels_hbm, lab, load_sem.at[1])
    big = [
        pltpu.make_async_copy(
            z_hbm.at[pl.ds(i * per, per)], z.at[pl.ds(i * per, per)], load_sem.at[2 + i]
        )
        for i in range(ZCHUNKS)
    ]
    res_copy.start()
    for copy in big:
        copy.start()
    lab_copy.start()
    level_copy = pltpu.make_async_copy(levels_hbm, levels, load_sem.at[2 + ZCHUNKS])
    level_copy.start()

    halves = npln // 2
    odd, half = lax.rem(pln, 2), lax.div(pln, 2)
    near_count, near_me = 2 * nz, odd * nz + zc
    wide_count, wide_me = halves * ny * 2, (half * ny + yc) * 2 + core

    def offsets(*sizes):
        def hops(offset):
            return sum(min(step, size - step) for step, size in zip(offset, sizes))

        every = list(itertools.product(*(range(size) for size in sizes)))
        return sorted(every[1:], key=hops, reverse=True)

    near_peers = [
        (sub - 2 * zc + 2 * lax.rem(zc + step, nz), pln + flip * (1 - 2 * odd))
        for flip, step in offsets(2, nz)
    ]
    wide_peers = [
        (
            (lax.rem(yc + step, ny) * nz + zc) * 2 + (1 - core if other else core),
            npln - 1 - pln if flip else pln,
        )
        for flip, step, other in offsets(halves, ny, 2)
    ]
    ahead = (lax.rem(sub + 1, nsub), pln)
    behind = (lax.rem(sub + nsub - 1, nsub), pln)
    right = (sub, lax.rem(pln + 1, npln))
    left = (sub, lax.rem(pln + npln - 1, npln))
    across = [(sub, lax.rem(pln + off, npln)) for off in (2, 1, 3) if off < npln]

    def beside(axis, steps):
        if axis == 0:
            return [
                (sub + 2 * (lax.rem(zc + step, nz) - zc), pln) for step in (steps, nz - steps)
            ]
        return [
            (sub + 2 * nz * (lax.rem(yc + step, ny) - yc), pln) for step in (steps, ny - steps)
        ]

    others = [ahead, behind] + across + beside(0, 1) + beside(1, 1)
    reaches = [[1 << i for i in range((size // 2).bit_length() - 1)] for size in (nz, ny)]

    def tokens_send(turn):
        for axis, reach in enumerate(reaches):
            if turn < len(reach):
                for peer in beside(axis, reach[turn]):
                    pl.semaphore_signal(
                        token.at[axis, turn], inc=1, device_id=peer, device_id_type=MESH
                    )

    def tokens_wait(turn):
        for axis, reach in enumerate(reaches):
            if turn < len(reach):
                pl.semaphore_wait(token.at[axis, turn], 2)

    turns = max(len(reach) for reach in reaches)

    barrier = pltpu.get_barrier_semaphore()
    for peer in others:
        pl.semaphore_signal(barrier, inc=1, device_id=peer, device_id_type=MESH)

    def remote(src, dst, send, recv, target):
        return pltpu.make_async_remote_copy(
            src_ref=src, dst_ref=dst, send_sem=send, recv_sem=recv,
            device_id=target, device_id_type=MESH,
        )

    pending = []

    def plane_copies(which, src, dst):
        copies = [
            remote(src.at[planes - 1], dst.at[0], side_send.at[which, 0],
                   side_recv.at[which, 0], right),
            remote(src.at[0], dst.at[1], side_send.at[which, 1], side_recv.at[which, 1], left),
        ]
        pending.extend(copies)
        return copies

    def edge_copies(which):
        copies = [
            remote(edge_send.at[which], edge.at[which, i], side_send.at[which, 2 + i],
                   side_recv.at[which, 2 + i], target)
            for i, target in enumerate((ahead, behind))
        ]
        pending.extend(copies)
        return copies

    def rows_send(which, row):
        rows[which, pln] = row
        mine = rows.at[which, pln]
        for peer in across:
            remote(mine, mine, row_send.at[which], row_recv.at[which], peer).start()

    def rows_wait(which):
        both = rows.at[which, pl.ds(0, npln - 1)]
        pltpu.make_async_copy(both, both, row_recv.at[which]).wait()
        result = rows[which, 0]
        for i in range(1, npln):
            result = result + rows[which, i]
        return result

    lane = lax.broadcasted_iota(jnp.int32, (1, depth), 1)
    lane8 = lax.broadcasted_iota(jnp.int32, (8, depth), 1)

    def across_lanes(value):
        return jnp.sum(value, axis=1, keepdims=True)

    def whole(value):
        slim = jnp.sum(value.reshape(-1, 8, depth), axis=0)
        return across_lanes(jnp.sum(slim, axis=0, keepdims=True))

    def tile_of(value, j):
        row = (j % per_plane) * 8
        return value[j // per_plane, row:row + 8, :]

    def pack_edges(value):
        packed = jnp.zeros((8, depth), jnp.float32)
        for j in range(tiles):
            rolled = pltpu.roll(tile_of(value, j), 2 * j + 1, 1)
            packed = jnp.where(lane8 // 2 == j, rolled, packed)
        return packed

    def unpack_behind(packed):
        pieces = [pltpu.roll(packed, (depth - 2 * j) % depth, 1) for j in range(tiles)]
        return jnp.concatenate(pieces, axis=0).reshape(planes, height, depth)

    def unpack_ahead(packed):
        pieces = [pltpu.roll(packed, depth - 2 - 2 * j, 1) for j in range(tiles)]
        return jnp.concatenate(pieces, axis=0).reshape(planes, height, depth)

    def project_some(value, start, stop):
        @pl.loop(start // STEP, stop // STEP)
        def _(block):
            for inner in range(STEP):
                k = block * STEP + inner
                product = z[k].astype(jnp.float32) * value
                slim = jnp.sum(product.reshape(-1, 8, depth), axis=0)
                part[pl.ds(k, 1), :] = jnp.sum(slim, axis=0, keepdims=True)

    def project_row():
        ones = jnp.ones((8, depth), jnp.float32)
        gathered = lax.dot_general(
            ones, part[...], (((1,), (1,)), ((), ())), precision=PRECISE,
            preferred_element_type=jnp.float32,
        )
        row = gathered[:1]
        return jnp.concatenate([row, jnp.zeros((1, depth - modes), jnp.float32)], axis=1)

    def spread_row(row):
        here = lax.broadcasted_iota(jnp.int32, (modes, depth), 0)
        there = lax.broadcasted_iota(jnp.int32, (modes, depth), 1)
        picked = jnp.where(here == there, jnp.broadcast_to(row, (modes, depth)), 0.0)
        spread[...] = jnp.broadcast_to(across_lanes(picked), (modes, depth))

    def expand_edges():
        def some(block, acc):
            for inner in range(8):
                k = block * 8 + inner
                acc = acc + edge_modes[k] * jnp.broadcast_to(spread[pl.ds(k, 1), :], (8, depth))
            return acc

        return lax.fori_loop(0, modes // 8, some, jnp.zeros((8, depth), jnp.float32))

    def expand_plane(plane):
        def some(block, acc):
            for inner in range(STEP):
                k = block * STEP + inner
                scale = jnp.broadcast_to(spread[pl.ds(k, 1), :], (height, depth))
                acc = acc + z[k, plane].astype(jnp.float32) * scale
            return acc

        return lax.fori_loop(0, modes // STEP, some, jnp.zeros((height, depth), jnp.float32))

    def expand(which, row):
        spread_row(row)
        edge_send[which + 1] = expand_edges()
        edges = edge_copies(which + 1)
        for copy in edges:
            copy.start()
        sides_x = plane_copies(which + 1, field_send.at[which], field_x.at[which])
        for plane in range(planes):
            value = expand_plane(plane)
            field[which, plane] = value
            field_send[which, plane] = value.astype(jnp.bfloat16)
            if plane == 0:
                sides_x[1].start()
        sides_x[0].start()
        return edges + sides_x

    y_index = lax.broadcasted_iota(jnp.int32, (planes, height, depth), 1)
    z_index = lax.broadcasted_iota(jnp.int32, (planes, height, depth), 2)

    def along_z(value, before, after):
        low = jnp.where(z_index == 0, unpack_behind(before), pltpu.roll(value, 1, 2))
        high = jnp.where(
            z_index == depth - 1, unpack_ahead(after), pltpu.roll(value, depth - 1, 2)
        )
        return low, high

    def stencil(which):
        value = field[which]
        zero = jnp.zeros_like(value)
        x_low = jnp.where(first_pln, 0.0, field_x[which, 0].astype(jnp.float32))
        x_high = jnp.where(last_pln, 0.0, field_x[which, 1].astype(jnp.float32))
        x_below = jnp.concatenate([x_low[None], value[:-1]], axis=0)
        x_above = jnp.concatenate([value[1:], x_high[None]], axis=0)
        y_below = jnp.where(y_index == 0, zero, pltpu.roll(value, 1, 1))
        y_above = jnp.where(y_index == height - 1, zero, pltpu.roll(value, height - 1, 1))
        z_below, z_above = along_z(value, edge[which + 1, 0], edge[which + 1, 1])
        return (
            wts[0] * (value - x_below)
            + wts[1] * (value - x_above)
            + wts[2] * (value - y_below)
            + wts[3] * (value - y_above)
            + wts[4] * (value - z_below)
            + wts[5] * (value - z_above)
        )

    res_copy.wait()
    for i in range(ZCHUNKS):
        big[i].wait()
        project_some(res[...], i * per, (i + 1) * per)
    rhs_part = project_row()
    pl.semaphore_wait(barrier, len(others))
    rows_send(0, rhs_part)
    if turns > 0:
        tokens_send(0)

    lab_copy.wait()
    level_copy.wait()
    narrow = lab[...].astype(jnp.float32)
    lab_send[...] = narrow.astype(jnp.bfloat16)
    edge_send[0] = pack_edges(narrow)
    label_copies = edge_copies(0) + plane_copies(0, lab_send, lab_x)
    for copy in label_copies:
        copy.start()

    @pl.loop(0, modes // 8)
    def _(block):
        for inner in range(8):
            k = block * 8 + inner
            edge_modes[k] = pack_edges(z[k].astype(jnp.float32))

    def density(labels):
        value = jnp.full(labels.shape, levels[0], jnp.float32)
        for i in range(1, levels.shape[0]):
            value = jnp.where(labels == float(i), levels[i], value)
        return value

    rhs = rows_wait(0)
    copies = expand(0, rhs)
    for turn in range(1, turns):
        tokens_wait(turn - 1)
        tokens_send(turn)
    for copy in label_copies:
        copy.wait_recv()
    coef = density(lab[...].astype(jnp.float32))
    low = jnp.where(first_pln, coef[0], density(lab_x[0].astype(jnp.float32)))
    high = jnp.where(last_pln, coef[planes - 1], density(lab_x[1].astype(jnp.float32)))
    wts[0] = harmonic(coef, jnp.concatenate([low[None], coef[:-1]], axis=0))
    wts[1] = harmonic(coef, jnp.concatenate([coef[1:], high[None]], axis=0))
    wts[2] = harmonic(coef, jnp.where(y_index == 0, coef, pltpu.roll(coef, 1, 1)))
    wts[3] = harmonic(
        coef, jnp.where(y_index == height - 1, coef, pltpu.roll(coef, height - 1, 1))
    )
    z_low, z_high = along_z(coef, density(edge[0, 0]), density(edge[0, 1]))
    wts[4] = harmonic(coef, z_low)
    wts[5] = harmonic(coef, z_high)

    for copy in copies:
        copy.wait_recv()
    image = stencil(0)
    project_some(image, 0, modes)
    if turns > 0:
        tokens_wait(turns - 1)
    rows_send(1, project_row())

    image_row = rows_wait(1)
    copies = expand(1, image_row)
    dq = across_lanes(rhs * image_row)
    qq = across_lanes(image_row * image_row)
    guess = jnp.where(qq > 0.0, dq / jnp.where(qq > 0.0, qq, 1.0), 0.0)
    rest = rhs - guess * image_row
    shared = {
        RR: across_lanes(rhs * rhs),
        DQ: dq,
        UU: across_lanes(rest * rest),
        UQ: across_lanes(rest * image_row),
        QQ: qq,
    }
    spot = lane - SLOT * zc
    packet = jnp.zeros((1, depth), jnp.float32)
    for i, value in shared.items():
        packet = jnp.where(spot == i, jnp.where(first_pln, value, 0.0), packet)
    guesses = jnp.where(
        jnp.logical_and(spot >= 0, spot < SLOT), jnp.where(first_pln, guess, 0.0), 0.0
    )
    for copy in copies:
        copy.wait_recv()
    image_next = stencil(1)
    guess3 = guess[:, :, None]
    rest_field = field[0] - guess3 * field[1]
    rest_image = image - guess3 * image_next
    local = {
        S1: whole(rest_field * rest_image),
        S2: whole(rest_field * image_next + field[1] * rest_image),
        S3: whole(field[1] * image_next),
    }
    for i, value in local.items():
        packet = jnp.where(spot == i, value, packet)

    near[near_me] = jnp.concatenate([packet, guesses], axis=0)
    mine = near.at[near_me]
    for peer in near_peers:
        remote(mine, mine, sum_send.at[0], sum_recv.at[0], peer).start()
    both = near.at[pl.ds(0, near_count - 1)]
    pltpu.make_async_copy(both, both, sum_recv.at[0]).wait()
    wide[wide_me] = jnp.sum(near[...], axis=0)
    mine = wide.at[wide_me]
    for peer in wide_peers:
        remote(mine, mine, sum_send.at[1], sum_recv.at[1], peer).start()
    both = wide.at[pl.ds(0, wide_count - 1)]
    pltpu.make_async_copy(both, both, sum_recv.at[1]).wait()
    count = wide_count // halves
    pairs = []
    for i in range(count):
        pair = wide[i]
        for j in range(1, halves):
            pair = pair + wide[j * count + i]
        pairs.append(pair)
    table = jnp.concatenate(pairs, axis=0)
    shape = table.shape
    upper = lax.broadcasted_iota(jnp.int32, shape, 0) % 2 == 0
    kind = jnp.where(upper, lax.broadcasted_iota(jnp.int32, shape, 1) % SLOT, SLOT)
    step_guess = pltpu.roll(table, shape[0] - 1, 0)

    def total(value):
        return across_lanes(jnp.sum(value, axis=0, keepdims=True))

    norm = total(jnp.where(kind == RR, table, 0.0))
    curve = total(jnp.where(kind == DQ, table, 0.0))
    alpha = norm / curve
    delta = alpha - step_guess
    squared = delta * delta * table
    norm_next = total(
        jnp.where(kind == UU, table, 0.0)
        + jnp.where(kind == UQ, -2.0 * delta * table, 0.0)
        + jnp.where(kind == QQ, squared, 0.0)
    )
    curve_rest = total(
        jnp.where(kind == S1, table, 0.0)
        + jnp.where(kind == S2, -delta * table, 0.0)
        + jnp.where(kind == S3, squared, 0.0)
    )
    mixed = total(
        jnp.where(kind == UQ, table, 0.0) + jnp.where(kind == QQ, -delta * table, 0.0)
    )
    beta = norm_next / norm
    curve_next = curve_rest + 2.0 * beta * mixed + beta * beta * curve
    alpha_next = norm_next / curve_next
    first_part = alpha + alpha_next * (1.0 + beta)
    second_part = alpha_next * alpha
    solution_row = first_part * rhs - second_part * image_row
    sol_ref[...] = solution_row[:, :modes]
    defl_ref[...] = (
        res[...] - first_part[:, :, None] * image + second_part[:, :, None] * image_next
    )

    for copy in pending:
        copy.wait_send()
    for which in range(2):
        both = rows.at[which, pl.ds(0, npln - 1)]
        pltpu.make_async_copy(both, both, row_send.at[which]).wait()
    both = near.at[pl.ds(0, near_count - 1)]
    pltpu.make_async_copy(both, both, sum_send.at[0]).wait()
    both = wide.at[pl.ds(0, wide_count - 1)]
    pltpu.make_async_copy(both, both, sum_send.at[1]).wait()


def finish(row, out, sol_hbm, defl_hbm, sems):
    copies = [
        pltpu.make_async_copy(out, defl_hbm, sems.at[0]),
        pltpu.make_async_copy(row, sol_hbm, sems.at[1]),
    ]
    for copy in copies:
        copy.start()
    for copy in copies:
        copy.wait()


def body(sides, labels, levels, zvec, resid):
    modes = zvec.shape[0]
    block = resid.shape
    ny, nz, npln = sides
    lanes = block[-1]
    in_hbm = pl.BlockSpec(memory_space=pltpu.HBM)
    vmem = pl.BlockSpec(memory_space=pltpu.VMEM)
    dma = pltpu.SemaphoreType.DMA
    wide = jnp.float32
    row, out = pl.pallas_call(
        functools.partial(kernel, sides),
        out_shape=(
            jax.ShapeDtypeStruct((1, modes), wide),
            jax.ShapeDtypeStruct(block, wide),
        ),
        in_specs=[in_hbm] * 4,
        out_specs=(vmem, vmem),
        scratch_shapes=[
            pltpu.VMEM(zvec.shape, zvec.dtype),
            pltpu.VMEM(block, labels.dtype),
            pltpu.VMEM(block, wide),
            pltpu.VMEM(block, jnp.bfloat16),
            pltpu.VMEM((2,) + block[1:], jnp.bfloat16),
            pltpu.VMEM((2,) + block, wide),
            pltpu.VMEM((2,) + block, jnp.bfloat16),
            pltpu.VMEM((2, 2) + block[1:], jnp.bfloat16),
            pltpu.VMEM((3, 8, lanes), wide),
            pltpu.VMEM((3, 2, 8, lanes), wide),
            pltpu.VMEM((modes, 8, lanes), wide),
            pltpu.VMEM((modes, lanes), wide),
            pltpu.VMEM((modes, lanes), wide),
            pltpu.VMEM((2, npln, 1, lanes), wide),
            pltpu.VMEM((2 * nz, 2, lanes), wide),
            pltpu.VMEM((npln * ny, 2, lanes), wide),
            pltpu.VMEM((6,) + block, wide),
            pltpu.SMEM(levels.shape, wide),
            dma((3 + ZCHUNKS,)),
            dma((3, 4)),
            dma((3, 4)),
            dma((2,)),
            dma((2,)),
            dma((2,)),
            dma((2,)),
            pltpu.SemaphoreType.REGULAR((2, 4)),
        ],
        compiler_params=pltpu.CompilerParams(
            collective_id=0, has_side_effects=True, vmem_limit_bytes=24 << 20
        ),
        name="deflated_coarse",
    )(
        *(pltpu.with_memory_space_constraint(a, pltpu.HBM) for a in (levels, labels, zvec, resid))
    )
    return pl.pallas_call(
        finish,
        out_shape=(
            jax.ShapeDtypeStruct((1, modes), wide),
            jax.ShapeDtypeStruct(block, wide),
        ),
        in_specs=[vmem, vmem],
        out_specs=(in_hbm, in_hbm),
        scratch_shapes=[dma((2,))],
        compiler_params=pltpu.CompilerParams(vmem_limit_bytes=2 << 20),
        name="finish",
    )(row, out)


def solution(mesh):
    chips = mesh.shape["sub"] // 2
    side = math.isqrt(chips)
    sides = (chips // side, side, mesh.shape["pln"])
    in_specs = (P("pln", None, "sub"), P(), P(None, "pln", None, "sub"), P("pln", None, "sub"))
    out_specs = (P("sub", None), P("pln", None, "sub"))
    return jax.shard_map(
        functools.partial(body, sides), mesh=mesh, in_specs=in_specs, out_specs=out_specs,
        check_vma=False,
    )
```

```python
import functools
import itertools
import math

import jax
import jax.numpy as jnp
from jax import lax
from jax.experimental import pallas as pl
from jax.experimental.pallas import tpu as pltpu
from jax.sharding import PartitionSpec as P

MESH = pl.DeviceIdType.MESH
PRECISE = lax.Precision.HIGHEST
ZCHUNKS = 8
STEP = 8
SLOT = 8
RR, DQ, UU, UQ, QQ, S1, S2, S3 = range(8)


def harmonic(left_value, right_value):
    return 2.0 * left_value * right_value / (left_value + right_value)


def kernel(
    sides,
    levels_hbm,
    labels_hbm,
    z_hbm,
    resid_hbm,
    sol_ref,
    defl_ref,
    z,
    zf,
    lab,
    res,
    lab_send,
    lab_x,
    field,
    field_send,
    field_x,
    edge_send,
    edge,
    edge_modes,
    spread,
    part,
    rows,
    near,
    wide,
    wts,
    levels,
    load_sem,
    side_send,
    side_recv,
    row_send,
    row_recv,
    sum_send,
    sum_recv,
    token,
):
    ny, nz, npln = sides
    nsub = ny * nz * 2
    modes, planes, height, depth = z.shape
    tiles = planes * height // 8
    per_plane = height // 8
    sub = lax.axis_index("sub")
    pln = lax.axis_index("pln")
    core = lax.rem(sub, 2)
    zc = lax.rem(lax.div(sub, 2), nz)
    yc = lax.div(sub, 2 * nz)
    first_pln = pln == 0
    last_pln = pln == npln - 1

    per = modes // ZCHUNKS
    res_copy = pltpu.make_async_copy(resid_hbm, res, load_sem.at[0])
    lab_copy = pltpu.make_async_copy(labels_hbm, lab, load_sem.at[1])
    big = [
        pltpu.make_async_copy(
            z_hbm.at[pl.ds(i * per, per)], z.at[pl.ds(i * per, per)], load_sem.at[2 + i]
        )
        for i in range(ZCHUNKS)
    ]
    res_copy.start()
    for copy in big:
        copy.start()
    lab_copy.start()
    level_copy = pltpu.make_async_copy(levels_hbm, levels, load_sem.at[2 + ZCHUNKS])
    level_copy.start()

    halves = npln // 2
    odd, half = lax.rem(pln, 2), lax.div(pln, 2)
    place = yc * 2 + core
    near_count, near_me = 4 * ny, odd * 2 * ny + place
    wide_count, wide_me = halves * nz, half * nz + zc

    def offsets(*sizes):
        def hops(offset):
            return sum(min(step, size - step) for step, size in zip(offset, sizes))

        every = list(itertools.product(*(range(size) for size in sizes)))
        return sorted(every[1:], key=hops, reverse=True)

    near_peers = [
        (
            (lax.rem(yc + step, ny) * nz + zc) * 2 + (1 - core if other else core),
            pln + flip * (1 - 2 * odd),
        )
        for flip, step, other in offsets(2, ny, 2)
    ]
    wide_peers = [
        (
            sub - 2 * zc + 2 * lax.rem(zc + step, nz),
            npln - 1 - pln if flip else pln,
        )
        for flip, step in offsets(halves, nz)
    ]
    ahead = (lax.rem(sub + 1, nsub), pln)
    behind = (lax.rem(sub + nsub - 1, nsub), pln)
    right = (sub, lax.rem(pln + 1, npln))
    left = (sub, lax.rem(pln + npln - 1, npln))
    across = [(sub, lax.rem(pln + off, npln)) for off in (2, 1, 3) if off < npln]

    def beside(axis, steps):
        if axis == 0:
            return [
                (sub + 2 * (lax.rem(zc + step, nz) - zc), pln) for step in (steps, nz - steps)
            ]
        return [
            (sub + 2 * nz * (lax.rem(yc + step, ny) - yc), pln) for step in (steps, ny - steps)
        ]

    others = [ahead, behind] + across + beside(0, 1) + beside(1, 1)
    reaches = [[1 << i for i in range((size // 2).bit_length() - 1)] for size in (nz, ny)]

    def tokens_send(turn):
        for axis, reach in enumerate(reaches):
            if turn < len(reach):
                for peer in beside(axis, reach[turn]):
                    pl.semaphore_signal(
                        token.at[axis, turn], inc=1, device_id=peer, device_id_type=MESH
                    )

    def tokens_wait(turn):
        for axis, reach in enumerate(reaches):
            if turn < len(reach):
                pl.semaphore_wait(token.at[axis, turn], 2)

    turns = max(len(reach) for reach in reaches)

    barrier = pltpu.get_barrier_semaphore()
    for peer in others:
        pl.semaphore_signal(barrier, inc=1, device_id=peer, device_id_type=MESH)

    def remote(src, dst, send, recv, target):
        return pltpu.make_async_remote_copy(
            src_ref=src, dst_ref=dst, send_sem=send, recv_sem=recv,
            device_id=target, device_id_type=MESH,
        )

    pending = []

    def plane_copies(which, src, dst):
        copies = [
            remote(src.at[planes - 1], dst.at[0], side_send.at[which, 0],
                   side_recv.at[which, 0], right),
            remote(src.at[0], dst.at[1], side_send.at[which, 1], side_recv.at[which, 1], left),
        ]
        pending.extend(copies)
        return copies

    def edge_copies(which):
        copies = [
            remote(edge_send.at[which], edge.at[which, i], side_send.at[which, 2 + i],
                   side_recv.at[which, 2 + i], target)
            for i, target in enumerate((ahead, behind))
        ]
        pending.extend(copies)
        return copies

    def rows_send(which, row):
        rows[which, pln] = row
        mine = rows.at[which, pln]
        for peer in across:
            remote(mine, mine, row_send.at[which], row_recv.at[which], peer).start()

    def rows_wait(which):
        both = rows.at[which, pl.ds(0, npln - 1)]
        pltpu.make_async_copy(both, both, row_recv.at[which]).wait()
        result = rows[which, 0]
        for i in range(1, npln):
            result = result + rows[which, i]
        return result

    lane = lax.broadcasted_iota(jnp.int32, (1, depth), 1)
    lane8 = lax.broadcasted_iota(jnp.int32, (8, depth), 1)

    def across_lanes(value):
        return jnp.sum(value, axis=1, keepdims=True)

    def whole(value):
        slim = jnp.sum(value.reshape(-1, 8, depth), axis=0)
        return across_lanes(jnp.sum(slim, axis=0, keepdims=True))

    def tile_of(value, j):
        row = (j % per_plane) * 8
        return value[j // per_plane, row:row + 8, :]

    def pack_edges(value):
        packed = jnp.zeros((8, depth), jnp.float32)
        for j in range(tiles):
            rolled = pltpu.roll(tile_of(value, j), 2 * j + 1, 1)
            packed = jnp.where(lane8 // 2 == j, rolled, packed)
        return packed

    def unpack_behind(packed):
        pieces = [pltpu.roll(packed, (depth - 2 * j) % depth, 1) for j in range(tiles)]
        return jnp.concatenate(pieces, axis=0).reshape(planes, height, depth)

    def unpack_ahead(packed):
        pieces = [pltpu.roll(packed, depth - 2 - 2 * j, 1) for j in range(tiles)]
        return jnp.concatenate(pieces, axis=0).reshape(planes, height, depth)

    def project_some(source, value, start, stop):
        @pl.loop(start // STEP, stop // STEP)
        def _(block):
            for inner in range(STEP):
                k = block * STEP + inner
                product = source[k].astype(jnp.float32) * value
                slim = jnp.sum(product.reshape(-1, 8, depth), axis=0)
                part[pl.ds(k, 1), :] = jnp.sum(slim, axis=0, keepdims=True)

    def project_row():
        ones = jnp.ones((8, depth), jnp.float32)
        gathered = lax.dot_general(
            ones, part[...], (((1,), (1,)), ((), ())), precision=PRECISE,
            preferred_element_type=jnp.float32,
        )
        row = gathered[:1]
        return jnp.concatenate([row, jnp.zeros((1, depth - modes), jnp.float32)], axis=1)

    def spread_row(row):
        here = lax.broadcasted_iota(jnp.int32, (modes, depth), 0)
        there = lax.broadcasted_iota(jnp.int32, (modes, depth), 1)
        picked = jnp.where(here == there, jnp.broadcast_to(row, (modes, depth)), 0.0)
        spread[...] = jnp.broadcast_to(across_lanes(picked), (modes, depth))

    def expand_edges():
        def some(block, acc):
            for inner in range(8):
                k = block * 8 + inner
                acc = acc + edge_modes[k] * jnp.broadcast_to(spread[pl.ds(k, 1), :], (8, depth))
            return acc

        return lax.fori_loop(0, modes // 8, some, jnp.zeros((8, depth), jnp.float32))

    def expand_plane(plane):
        def some(block, acc):
            for inner in range(STEP):
                k = block * STEP + inner
                scale = jnp.broadcast_to(spread[pl.ds(k, 1), :], (height, depth))
                acc = acc + zf[k, plane] * scale
            return acc

        return lax.fori_loop(0, modes // STEP, some, jnp.zeros((height, depth), jnp.float32))

    def expand(which, row):
        spread_row(row)
        edges = edge_copies(which + 1)
        sides_x = plane_copies(which + 1, field_send.at[which], field_x.at[which])
        for plane in range(planes):
            value = expand_plane(plane)
            field[which, plane] = value
            field_send[which, plane] = value.astype(jnp.bfloat16)
            if plane == 0:
                sides_x[1].start()
        sides_x[0].start()
        edge_send[which + 1] = expand_edges()
        for copy in edges:
            copy.start()
        return edges + sides_x

    y_index = lax.broadcasted_iota(jnp.int32, (planes, height, depth), 1)
    z_index = lax.broadcasted_iota(jnp.int32, (planes, height, depth), 2)

    def along_z(value, before, after):
        low = jnp.where(z_index == 0, unpack_behind(before), pltpu.roll(value, 1, 2))
        high = jnp.where(
            z_index == depth - 1, unpack_ahead(after), pltpu.roll(value, depth - 1, 2)
        )
        return low, high

    def stencil(which):
        value = field[which]
        zero = jnp.zeros_like(value)
        x_low = jnp.where(first_pln, 0.0, field_x[which, 0].astype(jnp.float32))
        x_high = jnp.where(last_pln, 0.0, field_x[which, 1].astype(jnp.float32))
        x_below = jnp.concatenate([x_low[None], value[:-1]], axis=0)
        x_above = jnp.concatenate([value[1:], x_high[None]], axis=0)
        y_below = jnp.where(y_index == 0, zero, pltpu.roll(value, 1, 1))
        y_above = jnp.where(y_index == height - 1, zero, pltpu.roll(value, height - 1, 1))
        z_below, z_above = along_z(value, edge[which + 1, 0], edge[which + 1, 1])
        return (
            wts[0] * (value - x_below)
            + wts[1] * (value - x_above)
            + wts[2] * (value - y_below)
            + wts[3] * (value - y_above)
            + wts[4] * (value - z_below)
            + wts[5] * (value - z_above)
        )

    res_copy.wait()
    for i in range(ZCHUNKS):
        big[i].wait()
        project_some(z, res[...], i * per, (i + 1) * per)
    rhs_part = project_row()
    pl.semaphore_wait(barrier, len(others))
    rows_send(0, rhs_part)
    if turns > 0:
        tokens_send(0)

    lab_copy.wait()
    level_copy.wait()
    narrow = lab[...].astype(jnp.float32)
    lab_send[...] = narrow.astype(jnp.bfloat16)
    edge_send[0] = pack_edges(narrow)
    label_copies = edge_copies(0) + plane_copies(0, lab_send, lab_x)
    for copy in label_copies:
        copy.start()

    @pl.loop(0, modes // 8)
    def _(block):
        for inner in range(8):
            k = block * 8 + inner
            mode = z[k].astype(jnp.float32)
            zf[k] = mode
            edge_modes[k] = pack_edges(mode)

    def density(labels):
        value = jnp.full(labels.shape, levels[0], jnp.float32)
        for i in range(1, levels.shape[0]):
            value = jnp.where(labels == float(i), levels[i], value)
        return value

    rhs = rows_wait(0)
    copies = expand(0, rhs)
    for turn in range(1, turns):
        tokens_wait(turn - 1)
        tokens_send(turn)
    for copy in label_copies:
        copy.wait_recv()
    coef = density(lab[...].astype(jnp.float32))
    low = jnp.where(first_pln, coef[0], density(lab_x[0].astype(jnp.float32)))
    high = jnp.where(last_pln, coef[planes - 1], density(lab_x[1].astype(jnp.float32)))
    wts[0] = harmonic(coef, jnp.concatenate([low[None], coef[:-1]], axis=0))
    wts[1] = harmonic(coef, jnp.concatenate([coef[1:], high[None]], axis=0))
    wts[2] = harmonic(coef, jnp.where(y_index == 0, coef, pltpu.roll(coef, 1, 1)))
    wts[3] = harmonic(
        coef, jnp.where(y_index == height - 1, coef, pltpu.roll(coef, height - 1, 1))
    )
    z_low, z_high = along_z(coef, density(edge[0, 0]), density(edge[0, 1]))
    wts[4] = harmonic(coef, z_low)
    wts[5] = harmonic(coef, z_high)

    for copy in copies:
        copy.wait_recv()
    image = stencil(0)
    project_some(zf, image, 0, modes)
    if turns > 0:
        tokens_wait(turns - 1)
    rows_send(1, project_row())

    image_row = rows_wait(1)
    copies = expand(1, image_row)
    dq = across_lanes(rhs * image_row)
    qq = across_lanes(image_row * image_row)
    guess = jnp.where(qq > 0.0, dq / jnp.where(qq > 0.0, qq, 1.0), 0.0)
    rest = rhs - guess * image_row
    shared = {
        RR: across_lanes(rhs * rhs),
        DQ: dq,
        UU: across_lanes(rest * rest),
        UQ: across_lanes(rest * image_row),
        QQ: qq,
    }
    spot = lane - SLOT * place
    packet = jnp.zeros((1, depth), jnp.float32)
    for i, value in shared.items():
        packet = jnp.where(spot == i, jnp.where(first_pln, value, 0.0), packet)
    guesses = jnp.where(
        jnp.logical_and(spot >= 0, spot < SLOT), jnp.where(first_pln, guess, 0.0), 0.0
    )
    for copy in copies:
        copy.wait_recv()
    image_next = stencil(1)
    guess3 = guess[:, :, None]
    rest_field = field[0] - guess3 * field[1]
    rest_image = image - guess3 * image_next
    local = {
        S1: whole(rest_field * rest_image),
        S2: whole(rest_field * image_next + field[1] * rest_image),
        S3: whole(field[1] * image_next),
    }
    for i, value in local.items():
        packet = jnp.where(spot == i, value, packet)

    near[near_me] = jnp.concatenate([packet, guesses], axis=0)
    mine = near.at[near_me]
    for peer in near_peers:
        remote(mine, mine, sum_send.at[0], sum_recv.at[0], peer).start()
    both = near.at[pl.ds(0, near_count - 1)]
    pltpu.make_async_copy(both, both, sum_recv.at[0]).wait()
    wide[wide_me] = jnp.sum(near[...], axis=0)
    mine = wide.at[wide_me]
    for peer in wide_peers:
        remote(mine, mine, sum_send.at[1], sum_recv.at[1], peer).start()
    both = wide.at[pl.ds(0, wide_count - 1)]
    pltpu.make_async_copy(both, both, sum_recv.at[1]).wait()
    count = wide_count // halves
    pairs = []
    for i in range(count):
        pair = wide[i]
        for j in range(1, halves):
            pair = pair + wide[j * count + i]
        pairs.append(pair)
    table = jnp.concatenate(pairs, axis=0)
    shape = table.shape
    upper = lax.broadcasted_iota(jnp.int32, shape, 0) % 2 == 0
    kind = jnp.where(upper, lax.broadcasted_iota(jnp.int32, shape, 1) % SLOT, SLOT)
    step_guess = pltpu.roll(table, shape[0] - 1, 0)

    def total(value):
        return across_lanes(jnp.sum(value, axis=0, keepdims=True))

    norm = total(jnp.where(kind == RR, table, 0.0))
    curve = total(jnp.where(kind == DQ, table, 0.0))
    alpha = norm / curve
    delta = alpha - step_guess
    squared = delta * delta * table
    norm_next = total(
        jnp.where(kind == UU, table, 0.0)
        + jnp.where(kind == UQ, -2.0 * delta * table, 0.0)
        + jnp.where(kind == QQ, squared, 0.0)
    )
    curve_rest = total(
        jnp.where(kind == S1, table, 0.0)
        + jnp.where(kind == S2, -delta * table, 0.0)
        + jnp.where(kind == S3, squared, 0.0)
    )
    mixed = total(
        jnp.where(kind == UQ, table, 0.0) + jnp.where(kind == QQ, -delta * table, 0.0)
    )
    beta = norm_next / norm
    curve_next = curve_rest + 2.0 * beta * mixed + beta * beta * curve
    alpha_next = norm_next / curve_next
    first_part = alpha + alpha_next * (1.0 + beta)
    second_part = alpha_next * alpha
    solution_row = first_part * rhs - second_part * image_row
    sol_ref[...] = solution_row[:, :modes]
    defl_ref[...] = (
        res[...] - first_part[:, :, None] * image + second_part[:, :, None] * image_next
    )

    for copy in pending:
        copy.wait_send()
    for which in range(2):
        both = rows.at[which, pl.ds(0, npln - 1)]
        pltpu.make_async_copy(both, both, row_send.at[which]).wait()
    both = near.at[pl.ds(0, near_count - 1)]
    pltpu.make_async_copy(both, both, sum_send.at[0]).wait()
    both = wide.at[pl.ds(0, wide_count - 1)]
    pltpu.make_async_copy(both, both, sum_send.at[1]).wait()


def finish(row, out, sol_hbm, defl_hbm, sems):
    copies = [
        pltpu.make_async_copy(out, defl_hbm, sems.at[0]),
        pltpu.make_async_copy(row, sol_hbm, sems.at[1]),
    ]
    for copy in copies:
        copy.start()
    for copy in copies:
        copy.wait()


def body(sides, labels, levels, zvec, resid):
    modes = zvec.shape[0]
    block = resid.shape
    ny, nz, npln = sides
    lanes = block[-1]
    in_hbm = pl.BlockSpec(memory_space=pltpu.HBM)
    vmem = pl.BlockSpec(memory_space=pltpu.VMEM)
    dma = pltpu.SemaphoreType.DMA
    wide = jnp.float32
    row, out = pl.pallas_call(
        functools.partial(kernel, sides),
        out_shape=(
            jax.ShapeDtypeStruct((1, modes), wide),
            jax.ShapeDtypeStruct(block, wide),
        ),
        in_specs=[in_hbm] * 4,
        out_specs=(vmem, vmem),
        scratch_shapes=[
            pltpu.VMEM(zvec.shape, zvec.dtype),
            pltpu.VMEM(zvec.shape, wide),
            pltpu.VMEM(block, labels.dtype),
            pltpu.VMEM(block, wide),
            pltpu.VMEM(block, jnp.bfloat16),
            pltpu.VMEM((2,) + block[1:], jnp.bfloat16),
            pltpu.VMEM((2,) + block, wide),
            pltpu.VMEM((2,) + block, jnp.bfloat16),
            pltpu.VMEM((2, 2) + block[1:], jnp.bfloat16),
            pltpu.VMEM((3, 8, lanes), wide),
            pltpu.VMEM((3, 2, 8, lanes), wide),
            pltpu.VMEM((modes, 8, lanes), wide),
            pltpu.VMEM((modes, lanes), wide),
            pltpu.VMEM((modes, lanes), wide),
            pltpu.VMEM((2, npln, 1, lanes), wide),
            pltpu.VMEM((4 * ny, 2, lanes), wide),
            pltpu.VMEM((npln // 2 * nz, 2, lanes), wide),
            pltpu.VMEM((6,) + block, wide),
            pltpu.SMEM(levels.shape, wide),
            dma((3 + ZCHUNKS,)),
            dma((3, 4)),
            dma((3, 4)),
            dma((2,)),
            dma((2,)),
            dma((2,)),
            dma((2,)),
            pltpu.SemaphoreType.REGULAR((2, 4)),
        ],
        compiler_params=pltpu.CompilerParams(
            collective_id=0, has_side_effects=True, vmem_limit_bytes=24 << 20
        ),
        name="deflated_coarse",
    )(
        *(pltpu.with_memory_space_constraint(a, pltpu.HBM) for a in (levels, labels, zvec, resid))
    )
    return pl.pallas_call(
        finish,
        out_shape=(
            jax.ShapeDtypeStruct((1, modes), wide),
            jax.ShapeDtypeStruct(block, wide),
        ),
        in_specs=[vmem, vmem],
        out_specs=(in_hbm, in_hbm),
        scratch_shapes=[dma((2,))],
        compiler_params=pltpu.CompilerParams(vmem_limit_bytes=2 << 20),
        name="finish",
    )(row, out)


def solution(mesh):
    chips = mesh.shape["sub"] // 2
    side = math.isqrt(chips)
    sides = (chips // side, side, mesh.shape["pln"])
    in_specs = (P("pln", None, "sub"), P(), P(None, "pln", None, "sub"), P("pln", None, "sub"))
    out_specs = (P("sub", None), P("pln", None, "sub"))
    return jax.shard_map(
        functools.partial(body, sides), mesh=mesh, in_specs=in_specs, out_specs=out_specs,
        check_vma=False,
    )
```

```python
import functools
import itertools
import math

import jax
import jax.numpy as jnp
from jax import lax
from jax.experimental import pallas as pl
from jax.experimental.pallas import tpu as pltpu
from jax.sharding import PartitionSpec as P

MESH = pl.DeviceIdType.MESH
ZCHUNKS = 4
STEP = 16
SLOT = 8
RR, DQ, UU, UQ, QQ, S1, S2, S3 = range(8)


def harmonic(left_value, right_value):
    return 2.0 * left_value * right_value / (left_value + right_value)


def kernel(
    sides,
    levels_hbm,
    labels_hbm,
    z_hbm,
    resid_hbm,
    sol_ref,
    defl_ref,
    z,
    zf,
    lab,
    res,
    lab_send,
    lab_x,
    field,
    field_send,
    field_x,
    edge_send,
    edge,
    edge_modes,
    spread,
    part,
    rows,
    near,
    wide,
    wts,
    levels,
    load_sem,
    side_send,
    side_recv,
    row_send,
    row_recv,
    sum_send,
    sum_recv,
    token,
):
    ny, nz, npln = sides
    nsub = ny * nz * 2
    modes, planes, height, depth = z.shape
    tiles = planes * height // 8
    per_plane = height // 8
    sub = lax.axis_index("sub")
    pln = lax.axis_index("pln")
    core = lax.rem(sub, 2)
    zc = lax.rem(lax.div(sub, 2), nz)
    yc = lax.div(sub, 2 * nz)
    first_pln = pln == 0
    last_pln = pln == npln - 1

    per = modes // ZCHUNKS
    res_copy = pltpu.make_async_copy(resid_hbm, res, load_sem.at[0])
    lab_copy = pltpu.make_async_copy(labels_hbm, lab, load_sem.at[1])
    big = [
        pltpu.make_async_copy(
            z_hbm.at[pl.ds(i * per, per)], z.at[pl.ds(i * per, per)], load_sem.at[2 + i]
        )
        for i in range(ZCHUNKS)
    ]
    res_copy.start()
    for copy in big:
        copy.start()
    lab_copy.start()
    level_copy = pltpu.make_async_copy(levels_hbm, levels, load_sem.at[2 + ZCHUNKS])
    level_copy.start()

    halves = npln // 2
    odd, half = lax.rem(pln, 2), lax.div(pln, 2)
    place = yc * 2 + core
    near_count, near_me = 4 * ny, odd * 2 * ny + place
    wide_count, wide_me = halves * nz, half * nz + zc

    def offsets(*sizes):
        def hops(offset):
            return sum(min(step, size - step) for step, size in zip(offset, sizes))

        every = list(itertools.product(*(range(size) for size in sizes)))
        return sorted(every[1:], key=hops, reverse=True)

    near_peers = [
        (
            (lax.rem(yc + step, ny) * nz + zc) * 2 + (1 - core if other else core),
            pln + flip * (1 - 2 * odd),
        )
        for flip, step, other in offsets(2, ny, 2)
    ]
    wide_peers = [
        (
            sub - 2 * zc + 2 * lax.rem(zc + step, nz),
            npln - 1 - pln if flip else pln,
        )
        for flip, step in offsets(halves, nz)
    ]
    ahead = (lax.rem(sub + 1, nsub), pln)
    behind = (lax.rem(sub + nsub - 1, nsub), pln)
    right = (sub, lax.rem(pln + 1, npln))
    left = (sub, lax.rem(pln + npln - 1, npln))
    across = [(sub, lax.rem(pln + off, npln)) for off in (2, 1, 3) if off < npln]

    def beside(axis, steps):
        if axis == 0:
            return [
                (sub + 2 * (lax.rem(zc + step, nz) - zc), pln) for step in (steps, nz - steps)
            ]
        return [
            (sub + 2 * nz * (lax.rem(yc + step, ny) - yc), pln) for step in (steps, ny - steps)
        ]

    others = [ahead, behind] + across + beside(0, 1) + beside(1, 1)
    reaches = [[1 << i for i in range((size // 2).bit_length() - 1)] for size in (nz, ny)]

    def tokens_send(turn):
        for axis, reach in enumerate(reaches):
            if turn < len(reach):
                for peer in beside(axis, reach[turn]):
                    pl.semaphore_signal(
                        token.at[axis, turn], inc=1, device_id=peer, device_id_type=MESH
                    )

    def tokens_wait(turn):
        for axis, reach in enumerate(reaches):
            if turn < len(reach):
                pl.semaphore_wait(token.at[axis, turn], 2)

    turns = max(len(reach) for reach in reaches)

    barrier = pltpu.get_barrier_semaphore()
    for peer in others:
        pl.semaphore_signal(barrier, inc=1, device_id=peer, device_id_type=MESH)

    def remote(src, dst, send, recv, target):
        return pltpu.make_async_remote_copy(
            src_ref=src, dst_ref=dst, send_sem=send, recv_sem=recv,
            device_id=target, device_id_type=MESH,
        )

    pending = []

    def plane_copies(which, src, dst):
        copies = [
            remote(src.at[planes - 1], dst.at[0], side_send.at[which, 0],
                   side_recv.at[which, 0], right),
            remote(src.at[0], dst.at[1], side_send.at[which, 1], side_recv.at[which, 1], left),
        ]
        pending.extend(copies)
        return copies

    def edge_copies(which):
        copies = [
            remote(edge_send.at[which], edge.at[which, i], side_send.at[which, 2 + i],
                   side_recv.at[which, 2 + i], target)
            for i, target in enumerate((ahead, behind))
        ]
        pending.extend(copies)
        return copies

    def rows_send(which, row):
        rows[which, pln] = row
        mine = rows.at[which, pln]
        for peer in across:
            remote(mine, mine, row_send.at[which], row_recv.at[which], peer).start()

    def rows_wait(which):
        both = rows.at[which, pl.ds(0, npln - 1)]
        pltpu.make_async_copy(both, both, row_recv.at[which]).wait()
        result = rows[which, 0]
        for i in range(1, npln):
            result = result + rows[which, i]
        return result

    lane = lax.broadcasted_iota(jnp.int32, (1, depth), 1)
    lane8 = lax.broadcasted_iota(jnp.int32, (8, depth), 1)

    def across_lanes(value):
        return jnp.sum(value, axis=1, keepdims=True)

    def whole(value):
        slim = jnp.sum(value.reshape(-1, 8, depth), axis=0)
        return across_lanes(jnp.sum(slim, axis=0, keepdims=True))

    def tile_of(value, j):
        row = (j % per_plane) * 8
        return value[j // per_plane, row:row + 8, :]

    def pack_edges(value):
        packed = jnp.zeros((8, depth), jnp.float32)
        for j in range(tiles):
            rolled = pltpu.roll(tile_of(value, j), 2 * j + 1, 1)
            packed = jnp.where(lane8 // 2 == j, rolled, packed)
        return packed

    def unpack_behind(packed):
        pieces = [pltpu.roll(packed, (depth - 2 * j) % depth, 1) for j in range(tiles)]
        return jnp.concatenate(pieces, axis=0).reshape(planes, height, depth)

    def unpack_ahead(packed):
        pieces = [pltpu.roll(packed, depth - 2 - 2 * j, 1) for j in range(tiles)]
        return jnp.concatenate(pieces, axis=0).reshape(planes, height, depth)

    def project_some(source, value, start, stop):
        @pl.loop(start // STEP, stop // STEP)
        def _(block):
            for inner in range(STEP):
                k = block * STEP + inner
                product = source[k].astype(jnp.float32) * value
                slim = jnp.sum(product.reshape(-1, 8, depth), axis=0)
                part[pl.ds(pl.multiple_of(k * 8, 8), 8), :] = slim

    def project_row():
        value = part[pl.ds(0, modes, stride=8), :]
        for i in range(1, 8):
            value = value + part[pl.ds(i, modes, stride=8), :]
        pieces = []
        for _ in range(3):
            pieces.append(value.astype(jnp.bfloat16))
            value = value - pieces[-1].astype(jnp.float32)
        gathered = lax.dot_general(
            jnp.ones((8, 3 * depth), jnp.bfloat16),
            jnp.concatenate(pieces, axis=1),
            (((1,), (1,)), ((), ())),
            preferred_element_type=jnp.float32,
        )
        row = gathered[:1]
        return jnp.concatenate([row, jnp.zeros((1, depth - modes), jnp.float32)], axis=1)

    def spread_row(row):
        here = lax.broadcasted_iota(jnp.int32, (modes, depth), 0)
        there = lax.broadcasted_iota(jnp.int32, (modes, depth), 1)
        picked = jnp.where(here == there, jnp.broadcast_to(row, (modes, depth)), 0.0)
        spread[...] = jnp.broadcast_to(across_lanes(picked), (modes, depth))

    def expand_edges():
        def some(block, acc):
            for inner in range(8):
                k = block * 8 + inner
                acc = acc + edge_modes[k] * jnp.broadcast_to(spread[pl.ds(k, 1), :], (8, depth))
            return acc

        return lax.fori_loop(0, modes // 8, some, jnp.zeros((8, depth), jnp.float32))

    def expand_plane(plane):
        def some(block, acc):
            for inner in range(STEP):
                k = block * STEP + inner
                scale = jnp.broadcast_to(spread[pl.ds(k, 1), :], (height, depth))
                acc = acc + zf[k, plane] * scale
            return acc

        return lax.fori_loop(0, modes // STEP, some, jnp.zeros((height, depth), jnp.float32))

    def expand(which, row):
        spread_row(row)
        edges = edge_copies(which + 1)
        sides_x = plane_copies(which + 1, field_send.at[which], field_x.at[which])
        for plane in range(planes):
            value = expand_plane(plane)
            field[which, plane] = value
            field_send[which, plane] = value.astype(jnp.bfloat16)
            if plane == 0:
                sides_x[1].start()
        sides_x[0].start()
        edge_send[which + 1] = expand_edges()
        for copy in edges:
            copy.start()
        return edges + sides_x

    y_index = lax.broadcasted_iota(jnp.int32, (planes, height, depth), 1)
    z_index = lax.broadcasted_iota(jnp.int32, (planes, height, depth), 2)

    def along_z(value, before, after):
        low = jnp.where(z_index == 0, unpack_behind(before), pltpu.roll(value, 1, 2))
        high = jnp.where(
            z_index == depth - 1, unpack_ahead(after), pltpu.roll(value, depth - 1, 2)
        )
        return low, high

    def stencil(which):
        value = field[which]
        zero = jnp.zeros_like(value)
        x_low = jnp.where(first_pln, 0.0, field_x[which, 0].astype(jnp.float32))
        x_high = jnp.where(last_pln, 0.0, field_x[which, 1].astype(jnp.float32))
        x_below = jnp.concatenate([x_low[None], value[:-1]], axis=0)
        x_above = jnp.concatenate([value[1:], x_high[None]], axis=0)
        y_below = jnp.where(y_index == 0, zero, pltpu.roll(value, 1, 1))
        y_above = jnp.where(y_index == height - 1, zero, pltpu.roll(value, height - 1, 1))
        z_below, z_above = along_z(value, edge[which + 1, 0], edge[which + 1, 1])
        return (
            wts[0] * (value - x_below)
            + wts[1] * (value - x_above)
            + wts[2] * (value - y_below)
            + wts[3] * (value - y_above)
            + wts[4] * (value - z_below)
            + wts[5] * (value - z_above)
        )

    res_copy.wait()
    for i in range(ZCHUNKS):
        big[i].wait()
        project_some(z, res[...], i * per, (i + 1) * per)
    rhs_part = project_row()
    pl.semaphore_wait(barrier, len(others))
    rows_send(0, rhs_part)
    if turns > 0:
        tokens_send(0)

    lab_copy.wait()
    level_copy.wait()
    narrow = lab[...].astype(jnp.float32)
    lab_send[...] = narrow.astype(jnp.bfloat16)
    edge_send[0] = pack_edges(narrow)
    label_copies = edge_copies(0) + plane_copies(0, lab_send, lab_x)
    for copy in label_copies:
        copy.start()

    @pl.loop(0, modes // 8)
    def _(block):
        for inner in range(8):
            k = block * 8 + inner
            mode = z[k].astype(jnp.float32)
            zf[k] = mode
            edge_modes[k] = pack_edges(mode)

    def density(labels):
        value = jnp.full(labels.shape, levels[0], jnp.float32)
        for i in range(1, levels.shape[0]):
            value = jnp.where(labels == float(i), levels[i], value)
        return value

    rhs = rows_wait(0)
    copies = expand(0, rhs)
    for turn in range(1, turns):
        tokens_wait(turn - 1)
        tokens_send(turn)
    for copy in label_copies:
        copy.wait_recv()
    coef = density(lab[...].astype(jnp.float32))
    low = jnp.where(first_pln, coef[0], density(lab_x[0].astype(jnp.float32)))
    high = jnp.where(last_pln, coef[planes - 1], density(lab_x[1].astype(jnp.float32)))
    wts[0] = harmonic(coef, jnp.concatenate([low[None], coef[:-1]], axis=0))
    wts[1] = harmonic(coef, jnp.concatenate([coef[1:], high[None]], axis=0))
    wts[2] = harmonic(coef, jnp.where(y_index == 0, coef, pltpu.roll(coef, 1, 1)))
    wts[3] = harmonic(
        coef, jnp.where(y_index == height - 1, coef, pltpu.roll(coef, height - 1, 1))
    )
    z_low, z_high = along_z(coef, density(edge[0, 0]), density(edge[0, 1]))
    wts[4] = harmonic(coef, z_low)
    wts[5] = harmonic(coef, z_high)

    for copy in copies:
        copy.wait_recv()
    image = stencil(0)
    project_some(zf, image, 0, modes)
    if turns > 0:
        tokens_wait(turns - 1)
    rows_send(1, project_row())

    image_row = rows_wait(1)
    copies = expand(1, image_row)
    dq = across_lanes(rhs * image_row)
    qq = across_lanes(image_row * image_row)
    guess = jnp.where(qq > 0.0, dq / jnp.where(qq > 0.0, qq, 1.0), 0.0)
    rest = rhs - guess * image_row
    shared = {
        RR: across_lanes(rhs * rhs),
        DQ: dq,
        UU: across_lanes(rest * rest),
        UQ: across_lanes(rest * image_row),
        QQ: qq,
    }
    spot = lane - SLOT * place
    packet = jnp.zeros((1, depth), jnp.float32)
    for i, value in shared.items():
        packet = jnp.where(spot == i, jnp.where(first_pln, value, 0.0), packet)
    guesses = jnp.where(
        jnp.logical_and(spot >= 0, spot < SLOT), jnp.where(first_pln, guess, 0.0), 0.0
    )
    for copy in copies:
        copy.wait_recv()
    image_next = stencil(1)
    guess3 = guess[:, :, None]
    rest_field = field[0] - guess3 * field[1]
    rest_image = image - guess3 * image_next
    local = {
        S1: whole(rest_field * rest_image),
        S2: whole(rest_field * image_next + field[1] * rest_image),
        S3: whole(field[1] * image_next),
    }
    for i, value in local.items():
        packet = jnp.where(spot == i, value, packet)

    near[near_me] = jnp.concatenate([packet, guesses], axis=0)
    mine = near.at[near_me]
    for peer in near_peers:
        remote(mine, mine, sum_send.at[0], sum_recv.at[0], peer).start()
    both = near.at[pl.ds(0, near_count - 1)]
    pltpu.make_async_copy(both, both, sum_recv.at[0]).wait()
    wide[wide_me] = jnp.sum(near[...], axis=0)
    mine = wide.at[wide_me]
    for peer in wide_peers:
        remote(mine, mine, sum_send.at[1], sum_recv.at[1], peer).start()
    for copy in pending:
        copy.wait_send()
    for which in range(2):
        both = rows.at[which, pl.ds(0, npln - 1)]
        pltpu.make_async_copy(both, both, row_send.at[which]).wait()
    both = near.at[pl.ds(0, near_count - 1)]
    pltpu.make_async_copy(both, both, sum_send.at[0]).wait()

    both = wide.at[pl.ds(0, wide_count - 1)]
    pltpu.make_async_copy(both, both, sum_recv.at[1]).wait()
    count = wide_count // halves
    pairs = []
    for i in range(count):
        pair = wide[i]
        for j in range(1, halves):
            pair = pair + wide[j * count + i]
        pairs.append(pair)
    table = jnp.concatenate(pairs, axis=0)
    shape = table.shape
    upper = lax.broadcasted_iota(jnp.int32, shape, 0) % 2 == 0
    kind = jnp.where(upper, lax.broadcasted_iota(jnp.int32, shape, 1) % SLOT, SLOT)
    step_guess = pltpu.roll(table, shape[0] - 1, 0)

    def total(value):
        return across_lanes(jnp.sum(value, axis=0, keepdims=True))

    norm = total(jnp.where(kind == RR, table, 0.0))
    curve = total(jnp.where(kind == DQ, table, 0.0))
    alpha = norm / curve
    delta = alpha - step_guess
    squared = delta * delta * table
    norm_next = total(
        jnp.where(kind == UU, table, 0.0)
        + jnp.where(kind == UQ, -2.0 * delta * table, 0.0)
        + jnp.where(kind == QQ, squared, 0.0)
    )
    curve_rest = total(
        jnp.where(kind == S1, table, 0.0)
        + jnp.where(kind == S2, -delta * table, 0.0)
        + jnp.where(kind == S3, squared, 0.0)
    )
    mixed = total(
        jnp.where(kind == UQ, table, 0.0) + jnp.where(kind == QQ, -delta * table, 0.0)
    )
    beta = norm_next / norm
    curve_next = curve_rest + 2.0 * beta * mixed + beta * beta * curve
    alpha_next = norm_next / curve_next
    first_part = alpha + alpha_next * (1.0 + beta)
    second_part = alpha_next * alpha
    solution_row = first_part * rhs - second_part * image_row
    sol_ref[...] = solution_row[:, :modes]
    defl_ref[...] = (
        res[...] - first_part[:, :, None] * image + second_part[:, :, None] * image_next
    )

    both = wide.at[pl.ds(0, wide_count - 1)]
    pltpu.make_async_copy(both, both, sum_send.at[1]).wait()


def finish(row, out, sol_hbm, defl_hbm, sems):
    copies = [
        pltpu.make_async_copy(out, defl_hbm, sems.at[0]),
        pltpu.make_async_copy(row, sol_hbm, sems.at[1]),
    ]
    for copy in copies:
        copy.start()
    for copy in copies:
        copy.wait()


def body(sides, labels, levels, zvec, resid):
    modes = zvec.shape[0]
    block = resid.shape
    ny, nz, npln = sides
    lanes = block[-1]
    in_hbm = pl.BlockSpec(memory_space=pltpu.HBM)
    vmem = pl.BlockSpec(memory_space=pltpu.VMEM)
    dma = pltpu.SemaphoreType.DMA
    wide = jnp.float32
    row, out = pl.pallas_call(
        functools.partial(kernel, sides),
        out_shape=(
            jax.ShapeDtypeStruct((1, modes), wide),
            jax.ShapeDtypeStruct(block, wide),
        ),
        in_specs=[in_hbm] * 4,
        out_specs=(vmem, vmem),
        scratch_shapes=[
            pltpu.VMEM(zvec.shape, zvec.dtype),
            pltpu.VMEM(zvec.shape, wide),
            pltpu.VMEM(block, labels.dtype),
            pltpu.VMEM(block, wide),
            pltpu.VMEM(block, jnp.bfloat16),
            pltpu.VMEM((2,) + block[1:], jnp.bfloat16),
            pltpu.VMEM((2,) + block, wide),
            pltpu.VMEM((2,) + block, jnp.bfloat16),
            pltpu.VMEM((2, 2) + block[1:], jnp.bfloat16),
            pltpu.VMEM((3, 8, lanes), wide),
            pltpu.VMEM((3, 2, 8, lanes), wide),
            pltpu.VMEM((modes, 8, lanes), wide),
            pltpu.VMEM((modes, lanes), wide),
            pltpu.VMEM((8 * modes, lanes), wide),
            pltpu.VMEM((2, npln, 1, lanes), wide),
            pltpu.VMEM((4 * ny, 2, lanes), wide),
            pltpu.VMEM((npln // 2 * nz, 2, lanes), wide),
            pltpu.VMEM((6,) + block, wide),
            pltpu.SMEM(levels.shape, wide),
            dma((3 + ZCHUNKS,)),
            dma((3, 4)),
            dma((3, 4)),
            dma((2,)),
            dma((2,)),
            dma((2,)),
            dma((2,)),
            pltpu.SemaphoreType.REGULAR((2, 4)),
        ],
        compiler_params=pltpu.CompilerParams(
            collective_id=0, has_side_effects=True, vmem_limit_bytes=24 << 20
        ),
        name="deflated_coarse",
    )(
        *(pltpu.with_memory_space_constraint(a, pltpu.HBM) for a in (levels, labels, zvec, resid))
    )
    return pl.pallas_call(
        finish,
        out_shape=(
            jax.ShapeDtypeStruct((1, modes), wide),
            jax.ShapeDtypeStruct(block, wide),
        ),
        in_specs=[vmem, vmem],
        out_specs=(in_hbm, in_hbm),
        scratch_shapes=[dma((2,))],
        compiler_params=pltpu.CompilerParams(vmem_limit_bytes=2 << 20),
        name="finish",
    )(row, out)


def solution(mesh):
    chips = mesh.shape["sub"] // 2
    side = math.isqrt(chips)
    sides = (chips // side, side, mesh.shape["pln"])
    in_specs = (P("pln", None, "sub"), P(), P(None, "pln", None, "sub"), P("pln", None, "sub"))
    out_specs = (P("sub", None), P("pln", None, "sub"))
    return jax.shard_map(
        functools.partial(body, sides), mesh=mesh, in_specs=in_specs, out_specs=out_specs,
        check_vma=False,
    )
```

```python
import functools
import itertools
import math

import jax
import jax.numpy as jnp
from jax import lax
from jax.experimental import pallas as pl
from jax.experimental.pallas import tpu as pltpu
from jax.sharding import PartitionSpec as P

MESH = pl.DeviceIdType.MESH
ZCHUNKS = 4
STEP = 16
SLOT = 8
RR, DQ, UU, UQ, QQ, S1, S2, S3 = range(8)


def harmonic(left_value, right_value):
    return 2.0 * left_value * right_value / (left_value + right_value)


def kernel(
    sides,
    levels_hbm,
    labels_hbm,
    z_hbm,
    resid_hbm,
    sol_ref,
    defl_ref,
    z,
    zf,
    lab,
    res,
    lab_send,
    lab_x,
    field,
    field_send,
    field_x,
    edge_send,
    edge,
    edge_modes,
    spread,
    part,
    rows,
    near,
    wide,
    wts,
    levels,
    load_sem,
    side_send,
    side_recv,
    row_send,
    row_recv,
    sum_send,
    sum_recv,
    token,
):
    ny, nz, npln = sides
    nsub = ny * nz * 2
    modes, planes, height, depth = z.shape
    tiles = planes * height // 8
    per_plane = height // 8
    sub = lax.axis_index("sub")
    pln = lax.axis_index("pln")
    core = lax.rem(sub, 2)
    zc = lax.rem(lax.div(sub, 2), nz)
    yc = lax.div(sub, 2 * nz)
    first_pln = pln == 0
    last_pln = pln == npln - 1

    per = modes // ZCHUNKS
    res_copy = pltpu.make_async_copy(resid_hbm, res, load_sem.at[0])
    lab_copy = pltpu.make_async_copy(labels_hbm, lab, load_sem.at[1])
    big = [
        pltpu.make_async_copy(
            z_hbm.at[pl.ds(i * per, per)], z.at[pl.ds(i * per, per)], load_sem.at[2 + i]
        )
        for i in range(ZCHUNKS)
    ]
    res_copy.start()
    for copy in big:
        copy.start()
    lab_copy.start()
    level_copy = pltpu.make_async_copy(levels_hbm, levels, load_sem.at[2 + ZCHUNKS])
    level_copy.start()

    halves = npln // 2
    odd, half = lax.rem(pln, 2), lax.div(pln, 2)
    place = yc * 2 + core
    near_count, near_me = 4 * ny, odd * 2 * ny + place
    wide_count, wide_me = halves * nz, half * nz + zc

    def offsets(*sizes):
        def hops(offset):
            return sum(min(step, size - step) for step, size in zip(offset, sizes))

        every = list(itertools.product(*(range(size) for size in sizes)))
        return sorted(every[1:], key=hops, reverse=True)

    near_peers = [
        (
            (lax.rem(yc + step, ny) * nz + zc) * 2 + (1 - core if other else core),
            pln + flip * (1 - 2 * odd),
        )
        for flip, step, other in offsets(2, ny, 2)
    ]
    wide_peers = [
        (
            sub - 2 * zc + 2 * lax.rem(zc + step, nz),
            npln - 1 - pln if flip else pln,
        )
        for flip, step in offsets(halves, nz)
    ]
    ahead = (lax.rem(sub + 1, nsub), pln)
    behind = (lax.rem(sub + nsub - 1, nsub), pln)
    right = (sub, lax.rem(pln + 1, npln))
    left = (sub, lax.rem(pln + npln - 1, npln))
    across = [(sub, lax.rem(pln + off, npln)) for off in (2, 1, 3) if off < npln]

    def beside(axis, steps):
        if axis == 0:
            return [
                (sub + 2 * (lax.rem(zc + step, nz) - zc), pln) for step in (steps, nz - steps)
            ]
        return [
            (sub + 2 * nz * (lax.rem(yc + step, ny) - yc), pln) for step in (steps, ny - steps)
        ]

    others = [ahead, behind] + across + beside(0, 1) + beside(1, 1)
    reaches = [[1 << i for i in range((size // 2).bit_length() - 1)] for size in (nz, ny)]

    def tokens_send(turn):
        for axis, reach in enumerate(reaches):
            if turn < len(reach):
                for peer in beside(axis, reach[turn]):
                    pl.semaphore_signal(
                        token.at[axis, turn], inc=1, device_id=peer, device_id_type=MESH
                    )

    def tokens_wait(turn):
        for axis, reach in enumerate(reaches):
            if turn < len(reach):
                pl.semaphore_wait(token.at[axis, turn], 2)

    turns = max(len(reach) for reach in reaches)

    barrier = pltpu.get_barrier_semaphore()
    for peer in others:
        pl.semaphore_signal(barrier, inc=1, device_id=peer, device_id_type=MESH)

    def remote(src, dst, send, recv, target):
        return pltpu.make_async_remote_copy(
            src_ref=src, dst_ref=dst, send_sem=send, recv_sem=recv,
            device_id=target, device_id_type=MESH,
        )

    pending = []

    def plane_copies(which, src, dst):
        copies = [
            remote(src.at[planes - 1], dst.at[0], side_send.at[which, 0],
                   side_recv.at[which, 0], right),
            remote(src.at[0], dst.at[1], side_send.at[which, 1], side_recv.at[which, 1], left),
        ]
        pending.extend(copies)
        return copies

    def edge_copies(which):
        copies = [
            remote(edge_send.at[which], edge.at[which, i], side_send.at[which, 2 + i],
                   side_recv.at[which, 2 + i], target)
            for i, target in enumerate((ahead, behind))
        ]
        pending.extend(copies)
        return copies

    def rows_send(which, row):
        rows[which, pln] = row
        mine = rows.at[which, pln]
        for peer in across:
            remote(mine, mine, row_send.at[which], row_recv.at[which], peer).start()

    def rows_wait(which):
        both = rows.at[which, pl.ds(0, npln - 1)]
        pltpu.make_async_copy(both, both, row_recv.at[which]).wait()
        result = rows[which, 0]
        for i in range(1, npln):
            result = result + rows[which, i]
        return result

    lane = lax.broadcasted_iota(jnp.int32, (1, depth), 1)
    lane8 = lax.broadcasted_iota(jnp.int32, (8, depth), 1)

    def across_lanes(value):
        return jnp.sum(value, axis=1, keepdims=True)

    def whole(value):
        slim = jnp.sum(value.reshape(-1, 8, depth), axis=0)
        return across_lanes(jnp.sum(slim, axis=0, keepdims=True))

    def tile_of(value, j):
        row = (j % per_plane) * 8
        return value[j // per_plane, row:row + 8, :]

    def pack_edges(value):
        packed = jnp.zeros((8, depth), jnp.float32)
        for j in range(tiles):
            rolled = pltpu.roll(tile_of(value, j), 2 * j + 1, 1)
            packed = jnp.where(lane8 // 2 == j, rolled, packed)
        return packed

    def unpack_behind(packed):
        pieces = [pltpu.roll(packed, (depth - 2 * j) % depth, 1) for j in range(tiles)]
        return jnp.concatenate(pieces, axis=0).reshape(planes, height, depth)

    def unpack_ahead(packed):
        pieces = [pltpu.roll(packed, depth - 2 - 2 * j, 1) for j in range(tiles)]
        return jnp.concatenate(pieces, axis=0).reshape(planes, height, depth)

    def project_some(source, value, start, stop):
        @pl.loop(start // STEP, stop // STEP)
        def _(block):
            for inner in range(STEP):
                k = block * STEP + inner
                product = source[k].astype(jnp.float32) * value
                slim = jnp.sum(product.reshape(-1, 8, depth), axis=0)
                part[pl.ds(k, 1), :] = jnp.sum(slim, axis=0, keepdims=True)

    def project_row():
        value = part[...]
        pieces = []
        for _ in range(3):
            pieces.append(value.astype(jnp.bfloat16))
            value = value - pieces[-1].astype(jnp.float32)
        gathered = lax.dot_general(
            jnp.ones((8, 3 * depth), jnp.bfloat16),
            jnp.concatenate(pieces, axis=1),
            (((1,), (1,)), ((), ())),
            preferred_element_type=jnp.float32,
        )
        row = gathered[:1]
        return jnp.concatenate([row, jnp.zeros((1, depth - modes), jnp.float32)], axis=1)

    def spread_row(row):
        here = lax.broadcasted_iota(jnp.int32, (modes, depth), 0)
        there = lax.broadcasted_iota(jnp.int32, (modes, depth), 1)
        picked = jnp.where(here == there, jnp.broadcast_to(row, (modes, depth)), 0.0)
        spread[...] = jnp.broadcast_to(across_lanes(picked), (modes, depth))

    def expand_edges():
        def some(block, acc):
            for inner in range(8):
                k = block * 8 + inner
                acc = acc + edge_modes[k] * jnp.broadcast_to(spread[pl.ds(k, 1), :], (8, depth))
            return acc

        return lax.fori_loop(0, modes // 8, some, jnp.zeros((8, depth), jnp.float32))

    def expand_plane(plane):
        def some(block, acc):
            for inner in range(STEP):
                k = block * STEP + inner
                scale = jnp.broadcast_to(spread[pl.ds(k, 1), :], (height, depth))
                acc = acc + zf[k, plane] * scale
            return acc

        return lax.fori_loop(0, modes // STEP, some, jnp.zeros((height, depth), jnp.float32))

    def expand(which, row):
        spread_row(row)
        edges = edge_copies(which + 1)
        sides_x = plane_copies(which + 1, field_send.at[which], field_x.at[which])
        for plane in range(planes):
            value = expand_plane(plane)
            field[which, plane] = value
            field_send[which, plane] = value.astype(jnp.bfloat16)
            if plane == 0:
                sides_x[1].start()
        sides_x[0].start()
        edge_send[which + 1] = expand_edges()
        for copy in edges:
            copy.start()
        return edges + sides_x

    y_index = lax.broadcasted_iota(jnp.int32, (planes, height, depth), 1)
    z_index = lax.broadcasted_iota(jnp.int32, (planes, height, depth), 2)

    def along_z(value, before, after):
        low = jnp.where(z_index == 0, unpack_behind(before), pltpu.roll(value, 1, 2))
        high = jnp.where(
            z_index == depth - 1, unpack_ahead(after), pltpu.roll(value, depth - 1, 2)
        )
        return low, high

    def stencil_inside(which):
        value = field[which]
        zero = jnp.zeros_like(value)
        edge_plane = jnp.zeros_like(value[:1])
        x_below = jnp.concatenate([edge_plane, value[:-1]], axis=0)
        x_above = jnp.concatenate([value[1:], edge_plane], axis=0)
        y_below = jnp.where(y_index == 0, zero, pltpu.roll(value, 1, 1))
        y_above = jnp.where(y_index == height - 1, zero, pltpu.roll(value, height - 1, 1))
        z_below = jnp.where(z_index == 0, zero, pltpu.roll(value, 1, 2))
        z_above = jnp.where(z_index == depth - 1, zero, pltpu.roll(value, depth - 1, 2))
        return (
            wts[0] * (value - x_below)
            + wts[1] * (value - x_above)
            + wts[2] * (value - y_below)
            + wts[3] * (value - y_above)
            + wts[4] * (value - z_below)
            + wts[5] * (value - z_above)
        )

    def stencil_sides(which, inside):
        x_low = jnp.where(first_pln, 0.0, field_x[which, 0].astype(jnp.float32))
        x_high = jnp.where(last_pln, 0.0, field_x[which, 1].astype(jnp.float32))
        z_below = unpack_behind(edge[which + 1, 0])
        z_above = unpack_ahead(edge[which + 1, 1])
        result = (
            inside
            - jnp.where(z_index == 0, wts[4] * z_below, 0.0)
            - jnp.where(z_index == depth - 1, wts[5] * z_above, 0.0)
        )
        top = planes - 1
        if top == 0:
            return result - (wts[0, 0] * x_low + wts[1, 0] * x_high)[None]
        first = result[0] - wts[0, 0] * x_low
        last = result[top] - wts[1, top] * x_high
        return jnp.concatenate([first[None], result[1:top], last[None]], axis=0) if top > 1 else (
            jnp.concatenate([first[None], last[None]], axis=0)
        )

    res_copy.wait()
    for i in range(ZCHUNKS):
        big[i].wait()
        project_some(z, res[...], i * per, (i + 1) * per)
    rhs_part = project_row()
    pl.semaphore_wait(barrier, len(others))
    rows_send(0, rhs_part)
    if turns > 0:
        tokens_send(0)

    lab_copy.wait()
    level_copy.wait()
    narrow = lab[...].astype(jnp.float32)
    lab_send[...] = narrow.astype(jnp.bfloat16)
    edge_send[0] = pack_edges(narrow)
    label_copies = edge_copies(0) + plane_copies(0, lab_send, lab_x)
    for copy in label_copies:
        copy.start()

    @pl.loop(0, modes // 8)
    def _(block):
        for inner in range(8):
            k = block * 8 + inner
            mode = z[k].astype(jnp.float32)
            zf[k] = mode
            edge_modes[k] = pack_edges(mode)

    def density(labels):
        value = jnp.full(labels.shape, levels[0], jnp.float32)
        for i in range(1, levels.shape[0]):
            value = jnp.where(labels == float(i), levels[i], value)
        return value

    rhs = rows_wait(0)
    copies = expand(0, rhs)
    for turn in range(1, turns):
        tokens_wait(turn - 1)
        tokens_send(turn)
    for copy in label_copies:
        copy.wait_recv()
    coef = density(lab[...].astype(jnp.float32))
    low = jnp.where(first_pln, coef[0], density(lab_x[0].astype(jnp.float32)))
    high = jnp.where(last_pln, coef[planes - 1], density(lab_x[1].astype(jnp.float32)))
    wts[0] = harmonic(coef, jnp.concatenate([low[None], coef[:-1]], axis=0))
    wts[1] = harmonic(coef, jnp.concatenate([coef[1:], high[None]], axis=0))
    wts[2] = harmonic(coef, jnp.where(y_index == 0, coef, pltpu.roll(coef, 1, 1)))
    wts[3] = harmonic(
        coef, jnp.where(y_index == height - 1, coef, pltpu.roll(coef, height - 1, 1))
    )
    z_low, z_high = along_z(coef, density(edge[0, 0]), density(edge[0, 1]))
    wts[4] = harmonic(coef, z_low)
    wts[5] = harmonic(coef, z_high)

    inside = stencil_inside(0)
    for copy in copies:
        copy.wait_recv()
    image = stencil_sides(0, inside)
    project_some(zf, image, 0, modes)
    if turns > 0:
        tokens_wait(turns - 1)
    rows_send(1, project_row())

    image_row = rows_wait(1)
    copies = expand(1, image_row)
    dq = across_lanes(rhs * image_row)
    qq = across_lanes(image_row * image_row)
    guess = jnp.where(qq > 0.0, dq / jnp.where(qq > 0.0, qq, 1.0), 0.0)
    rest = rhs - guess * image_row
    shared = {
        RR: across_lanes(rhs * rhs),
        DQ: dq,
        UU: across_lanes(rest * rest),
        UQ: across_lanes(rest * image_row),
        QQ: qq,
    }
    spot = lane - SLOT * place
    packet = jnp.zeros((1, depth), jnp.float32)
    for i, value in shared.items():
        packet = jnp.where(spot == i, jnp.where(first_pln, value, 0.0), packet)
    guesses = jnp.where(
        jnp.logical_and(spot >= 0, spot < SLOT), jnp.where(first_pln, guess, 0.0), 0.0
    )
    inside = stencil_inside(1)
    for copy in copies:
        copy.wait_recv()
    image_next = stencil_sides(1, inside)
    guess3 = guess[:, :, None]
    rest_field = field[0] - guess3 * field[1]
    rest_image = image - guess3 * image_next
    local = {
        S1: whole(rest_field * rest_image),
        S2: whole(rest_field * image_next + field[1] * rest_image),
        S3: whole(field[1] * image_next),
    }
    for i, value in local.items():
        packet = jnp.where(spot == i, value, packet)

    near[near_me] = jnp.concatenate([packet, guesses], axis=0)
    mine = near.at[near_me]
    for peer in near_peers:
        remote(mine, mine, sum_send.at[0], sum_recv.at[0], peer).start()
    both = near.at[pl.ds(0, near_count - 1)]
    pltpu.make_async_copy(both, both, sum_recv.at[0]).wait()
    wide[wide_me] = jnp.sum(near[...], axis=0)
    mine = wide.at[wide_me]
    for peer in wide_peers:
        remote(mine, mine, sum_send.at[1], sum_recv.at[1], peer).start()
    for copy in pending:
        copy.wait_send()
    for which in range(2):
        both = rows.at[which, pl.ds(0, npln - 1)]
        pltpu.make_async_copy(both, both, row_send.at[which]).wait()
    both = near.at[pl.ds(0, near_count - 1)]
    pltpu.make_async_copy(both, both, sum_send.at[0]).wait()

    both = wide.at[pl.ds(0, wide_count - 1)]
    pltpu.make_async_copy(both, both, sum_recv.at[1]).wait()
    count = wide_count // halves
    pairs = []
    for i in range(count):
        pair = wide[i]
        for j in range(1, halves):
            pair = pair + wide[j * count + i]
        pairs.append(pair)
    table = jnp.concatenate(pairs, axis=0)
    shape = table.shape
    upper = lax.broadcasted_iota(jnp.int32, shape, 0) % 2 == 0
    kind = jnp.where(upper, lax.broadcasted_iota(jnp.int32, shape, 1) % SLOT, SLOT)
    step_guess = pltpu.roll(table, shape[0] - 1, 0)

    def total(value):
        return across_lanes(jnp.sum(value, axis=0, keepdims=True))

    norm = total(jnp.where(kind == RR, table, 0.0))
    curve = total(jnp.where(kind == DQ, table, 0.0))
    alpha = norm / curve
    delta = alpha - step_guess
    squared = delta * delta * table
    norm_next = total(
        jnp.where(kind == UU, table, 0.0)
        + jnp.where(kind == UQ, -2.0 * delta * table, 0.0)
        + jnp.where(kind == QQ, squared, 0.0)
    )
    curve_rest = total(
        jnp.where(kind == S1, table, 0.0)
        + jnp.where(kind == S2, -delta * table, 0.0)
        + jnp.where(kind == S3, squared, 0.0)
    )
    mixed = total(
        jnp.where(kind == UQ, table, 0.0) + jnp.where(kind == QQ, -delta * table, 0.0)
    )
    beta = norm_next / norm
    curve_next = curve_rest + 2.0 * beta * mixed + beta * beta * curve
    alpha_next = norm_next / curve_next
    first_part = alpha + alpha_next * (1.0 + beta)
    second_part = alpha_next * alpha
    solution_row = first_part * rhs - second_part * image_row
    sol_ref[...] = solution_row[:, :modes]
    defl_ref[...] = (
        res[...] - first_part[:, :, None] * image + second_part[:, :, None] * image_next
    )

    both = wide.at[pl.ds(0, wide_count - 1)]
    pltpu.make_async_copy(both, both, sum_send.at[1]).wait()


def finish(row, out, sol_hbm, defl_hbm, sems):
    copies = [
        pltpu.make_async_copy(out, defl_hbm, sems.at[0]),
        pltpu.make_async_copy(row, sol_hbm, sems.at[1]),
    ]
    for copy in copies:
        copy.start()
    for copy in copies:
        copy.wait()


def body(sides, labels, levels, zvec, resid):
    modes = zvec.shape[0]
    block = resid.shape
    ny, nz, npln = sides
    lanes = block[-1]
    in_hbm = pl.BlockSpec(memory_space=pltpu.HBM)
    vmem = pl.BlockSpec(memory_space=pltpu.VMEM)
    dma = pltpu.SemaphoreType.DMA
    wide = jnp.float32
    row, out = pl.pallas_call(
        functools.partial(kernel, sides),
        out_shape=(
            jax.ShapeDtypeStruct((1, modes), wide),
            jax.ShapeDtypeStruct(block, wide),
        ),
        in_specs=[in_hbm] * 4,
        out_specs=(vmem, vmem),
        scratch_shapes=[
            pltpu.VMEM(zvec.shape, zvec.dtype),
            pltpu.VMEM(zvec.shape, wide),
            pltpu.VMEM(block, labels.dtype),
            pltpu.VMEM(block, wide),
            pltpu.VMEM(block, jnp.bfloat16),
            pltpu.VMEM((2,) + block[1:], jnp.bfloat16),
            pltpu.VMEM((2,) + block, wide),
            pltpu.VMEM((2,) + block, jnp.bfloat16),
            pltpu.VMEM((2, 2) + block[1:], jnp.bfloat16),
            pltpu.VMEM((3, 8, lanes), wide),
            pltpu.VMEM((3, 2, 8, lanes), wide),
            pltpu.VMEM((modes, 8, lanes), wide),
            pltpu.VMEM((modes, lanes), wide),
            pltpu.VMEM((modes, lanes), wide),
            pltpu.VMEM((2, npln, 1, lanes), wide),
            pltpu.VMEM((4 * ny, 2, lanes), wide),
            pltpu.VMEM((npln // 2 * nz, 2, lanes), wide),
            pltpu.VMEM((6,) + block, wide),
            pltpu.SMEM(levels.shape, wide),
            dma((3 + ZCHUNKS,)),
            dma((3, 4)),
            dma((3, 4)),
            dma((2,)),
            dma((2,)),
            dma((2,)),
            dma((2,)),
            pltpu.SemaphoreType.REGULAR((2, 4)),
        ],
        compiler_params=pltpu.CompilerParams(
            collective_id=0, has_side_effects=True, vmem_limit_bytes=24 << 20
        ),
        name="deflated_coarse",
    )(
        *(pltpu.with_memory_space_constraint(a, pltpu.HBM) for a in (levels, labels, zvec, resid))
    )
    return pl.pallas_call(
        finish,
        out_shape=(
            jax.ShapeDtypeStruct((1, modes), wide),
            jax.ShapeDtypeStruct(block, wide),
        ),
        in_specs=[vmem, vmem],
        out_specs=(in_hbm, in_hbm),
        scratch_shapes=[dma((2,))],
        compiler_params=pltpu.CompilerParams(vmem_limit_bytes=2 << 20),
        name="finish",
    )(row, out)


def solution(mesh):
    chips = mesh.shape["sub"] // 2
    side = math.isqrt(chips)
    sides = (chips // side, side, mesh.shape["pln"])
    in_specs = (P("pln", None, "sub"), P(), P(None, "pln", None, "sub"), P("pln", None, "sub"))
    out_specs = (P("sub", None), P("pln", None, "sub"))
    return jax.shard_map(
        functools.partial(body, sides), mesh=mesh, in_specs=in_specs, out_specs=out_specs,
        check_vma=False,
    )
```

```python
import functools
import itertools
import math

import jax
import jax.numpy as jnp
from jax import lax
from jax.experimental import pallas as pl
from jax.experimental.pallas import tpu as pltpu
from jax.sharding import PartitionSpec as P

MESH = pl.DeviceIdType.MESH
ZCHUNKS = 4
STEP = 16
SLOT = 8
RR, DQ, UU, UQ, QQ, S1, S2, S3 = range(8)


def harmonic(left_value, right_value):
    return 2.0 * left_value * right_value / (left_value + right_value)


def kernel(
    sides,
    levels_hbm,
    labels_hbm,
    z_hbm,
    resid_hbm,
    sol_ref,
    defl_ref,
    z,
    zf,
    lab,
    res,
    lab_send,
    lab_x,
    field,
    field_send,
    field_x,
    edge_send,
    edge,
    edge_modes,
    spread,
    part,
    rows,
    near,
    wide,
    wts,
    levels,
    load_sem,
    side_send,
    side_recv,
    row_send,
    row_recv,
    sum_send,
    sum_recv,
    token,
):
    ny, nz, npln = sides
    nsub = ny * nz * 2
    modes, planes, height, depth = z.shape
    tiles = planes * height // 8
    per_plane = height // 8
    sub = lax.axis_index("sub")
    pln = lax.axis_index("pln")
    core = lax.rem(sub, 2)
    zc = lax.rem(lax.div(sub, 2), nz)
    yc = lax.div(sub, 2 * nz)
    first_pln = pln == 0
    last_pln = pln == npln - 1

    per = modes // ZCHUNKS
    res_copy = pltpu.make_async_copy(resid_hbm, res, load_sem.at[0])
    lab_copy = pltpu.make_async_copy(labels_hbm, lab, load_sem.at[1])
    big = [
        pltpu.make_async_copy(
            z_hbm.at[pl.ds(i * per, per)], z.at[pl.ds(i * per, per)], load_sem.at[2 + i]
        )
        for i in range(ZCHUNKS)
    ]
    res_copy.start()
    for copy in big:
        copy.start()
    lab_copy.start()
    level_copy = pltpu.make_async_copy(levels_hbm, levels, load_sem.at[2 + ZCHUNKS])
    level_copy.start()

    halves = npln // 2
    odd, half = lax.rem(pln, 2), lax.div(pln, 2)
    place = yc * 2 + core
    near_count, near_me = 4 * ny, odd * 2 * ny + place
    wide_count, wide_me = halves * nz, half * nz + zc

    def offsets(*sizes):
        def hops(offset):
            return sum(min(step, size - step) for step, size in zip(offset, sizes))

        every = list(itertools.product(*(range(size) for size in sizes)))
        return sorted(every[1:], key=hops, reverse=True)

    near_peers = [
        (
            (lax.rem(yc + step, ny) * nz + zc) * 2 + (1 - core if other else core),
            pln + flip * (1 - 2 * odd),
        )
        for flip, step, other in offsets(2, ny, 2)
    ]
    wide_peers = [
        (
            sub - 2 * zc + 2 * lax.rem(zc + step, nz),
            npln - 1 - pln if flip else pln,
        )
        for flip, step in offsets(halves, nz)
    ]
    ahead = (lax.rem(sub + 1, nsub), pln)
    behind = (lax.rem(sub + nsub - 1, nsub), pln)
    right = (sub, lax.rem(pln + 1, npln))
    left = (sub, lax.rem(pln + npln - 1, npln))
    across = [(sub, lax.rem(pln + off, npln)) for off in (2, 1, 3) if off < npln]

    def beside(axis, steps):
        if axis == 0:
            return [
                (sub + 2 * (lax.rem(zc + step, nz) - zc), pln) for step in (steps, nz - steps)
            ]
        return [
            (sub + 2 * nz * (lax.rem(yc + step, ny) - yc), pln) for step in (steps, ny - steps)
        ]

    others = [ahead, behind] + across + beside(0, 1) + beside(1, 1)
    reaches = [[1 << i for i in range((size // 2).bit_length() - 1)] for size in (nz, ny)]

    def tokens_send(turn):
        for axis, reach in enumerate(reaches):
            if turn < len(reach):
                for peer in beside(axis, reach[turn]):
                    pl.semaphore_signal(
                        token.at[axis, turn], inc=1, device_id=peer, device_id_type=MESH
                    )

    def tokens_wait(turn):
        for axis, reach in enumerate(reaches):
            if turn < len(reach):
                pl.semaphore_wait(token.at[axis, turn], 2)

    turns = max(len(reach) for reach in reaches)

    barrier = pltpu.get_barrier_semaphore()
    for peer in others:
        pl.semaphore_signal(barrier, inc=1, device_id=peer, device_id_type=MESH)

    def remote(src, dst, send, recv, target):
        return pltpu.make_async_remote_copy(
            src_ref=src, dst_ref=dst, send_sem=send, recv_sem=recv,
            device_id=target, device_id_type=MESH,
        )

    pending = []

    def plane_copies(which, src, dst):
        copies = [
            remote(src.at[planes - 1], dst.at[0], side_send.at[which, 0],
                   side_recv.at[which, 0], right),
            remote(src.at[0], dst.at[1], side_send.at[which, 1], side_recv.at[which, 1], left),
        ]
        pending.extend(copies)
        return copies

    def edge_copies(which):
        copies = [
            remote(edge_send.at[which], edge.at[which, i], side_send.at[which, 2 + i],
                   side_recv.at[which, 2 + i], target)
            for i, target in enumerate((ahead, behind))
        ]
        pending.extend(copies)
        return copies

    def rows_send(which, row):
        rows[which, pln] = row
        mine = rows.at[which, pln]
        for peer in across:
            remote(mine, mine, row_send.at[which], row_recv.at[which], peer).start()

    def rows_wait(which):
        both = rows.at[which, pl.ds(0, npln - 1)]
        pltpu.make_async_copy(both, both, row_recv.at[which]).wait()
        result = rows[which, 0]
        for i in range(1, npln):
            result = result + rows[which, i]
        return result

    lane = lax.broadcasted_iota(jnp.int32, (1, depth), 1)
    lane8 = lax.broadcasted_iota(jnp.int32, (8, depth), 1)

    def across_lanes(value):
        return jnp.sum(value, axis=1, keepdims=True)

    def whole(value):
        slim = jnp.sum(value.reshape(-1, 8, depth), axis=0)
        return across_lanes(jnp.sum(slim, axis=0, keepdims=True))

    def tile_of(value, j):
        row = (j % per_plane) * 8
        return value[j // per_plane, row:row + 8, :]

    def pack_edges(value):
        packed = jnp.zeros((8, depth), jnp.float32)
        for j in range(tiles):
            rolled = pltpu.roll(tile_of(value, j), 2 * j + 1, 1)
            packed = jnp.where(lane8 // 2 == j, rolled, packed)
        return packed

    def unpack_behind(packed):
        pieces = [pltpu.roll(packed, (depth - 2 * j) % depth, 1) for j in range(tiles)]
        return jnp.concatenate(pieces, axis=0).reshape(planes, height, depth)

    def unpack_ahead(packed):
        pieces = [pltpu.roll(packed, depth - 2 - 2 * j, 1) for j in range(tiles)]
        return jnp.concatenate(pieces, axis=0).reshape(planes, height, depth)

    def project_some(source, value, start, stop):
        @pl.loop(start // STEP, stop // STEP)
        def _(block):
            for inner in range(STEP):
                k = block * STEP + inner
                product = source[k].astype(jnp.float32) * value
                slim = jnp.sum(product.reshape(-1, 8, depth), axis=0)
                part[pl.ds(k, 1), :] = jnp.sum(slim, axis=0, keepdims=True)

    def project_row():
        value = part[...]
        pieces = []
        for _ in range(3):
            pieces.append(value.astype(jnp.bfloat16))
            value = value - pieces[-1].astype(jnp.float32)
        gathered = lax.dot_general(
            jnp.ones((8, 3 * depth), jnp.bfloat16),
            jnp.concatenate(pieces, axis=1),
            (((1,), (1,)), ((), ())),
            preferred_element_type=jnp.float32,
        )
        row = gathered[:1]
        return jnp.concatenate([row, jnp.zeros((1, depth - modes), jnp.float32)], axis=1)

    def spread_row(row):
        here = lax.broadcasted_iota(jnp.int32, (modes, depth), 0)
        there = lax.broadcasted_iota(jnp.int32, (modes, depth), 1)
        picked = jnp.where(here == there, jnp.broadcast_to(row, (modes, depth)), 0.0)
        spread[...] = jnp.broadcast_to(across_lanes(picked), (modes, depth))

    def expand_edges():
        def some(block, acc):
            for inner in range(8):
                k = block * 8 + inner
                acc = acc + edge_modes[k] * jnp.broadcast_to(spread[pl.ds(k, 1), :], (8, depth))
            return acc

        return lax.fori_loop(0, modes // 8, some, jnp.zeros((8, depth), jnp.float32))

    def expand_part(plane, start, size):
        def some(block, acc):
            for inner in range(STEP):
                k = block * STEP + inner
                scale = jnp.broadcast_to(spread[pl.ds(k, 1), :], (size, depth))
                acc = acc + zf[k, plane, pl.ds(start, size)] * scale
            return acc

        return lax.fori_loop(0, modes // STEP, some, jnp.zeros((size, depth), jnp.float32))

    def expand(which, row):
        spread_row(row)
        edges = edge_copies(which + 1)
        size = height // 2
        sent = []
        for plane in range(planes):
            for i in range(2):
                span = pl.ds(i * size, size)
                value = expand_part(plane, i * size, size)
                field[which, plane, span] = value
                field_send[which, plane, span] = value.astype(jnp.bfloat16)
                mine = field_send.at[which, plane, span]
                for side, target in enumerate((right, left)):
                    if plane == (planes - 1 if side == 0 else 0):
                        spot = (which + 1, 4 + 2 * side + i)
                        copy = remote(mine, field_x.at[which, side, span], side_send.at[spot],
                                      side_recv.at[spot], target)
                        copy.start()
                        sent.append(copy)
        pending.extend(sent)
        edge_send[which + 1] = expand_edges()
        for copy in edges:
            copy.start()
        return edges + sent

    y_index = lax.broadcasted_iota(jnp.int32, (planes, height, depth), 1)
    z_index = lax.broadcasted_iota(jnp.int32, (planes, height, depth), 2)

    def along_z(value, before, after):
        low = jnp.where(z_index == 0, unpack_behind(before), pltpu.roll(value, 1, 2))
        high = jnp.where(
            z_index == depth - 1, unpack_ahead(after), pltpu.roll(value, depth - 1, 2)
        )
        return low, high

    def stencil_inside(which):
        value = field[which]
        zero = jnp.zeros_like(value)
        edge_plane = jnp.zeros_like(value[:1])
        x_below = jnp.concatenate([edge_plane, value[:-1]], axis=0)
        x_above = jnp.concatenate([value[1:], edge_plane], axis=0)
        y_below = jnp.where(y_index == 0, zero, pltpu.roll(value, 1, 1))
        y_above = jnp.where(y_index == height - 1, zero, pltpu.roll(value, height - 1, 1))
        z_below = jnp.where(z_index == 0, zero, pltpu.roll(value, 1, 2))
        z_above = jnp.where(z_index == depth - 1, zero, pltpu.roll(value, depth - 1, 2))
        return (
            wts[0] * (value - x_below)
            + wts[1] * (value - x_above)
            + wts[2] * (value - y_below)
            + wts[3] * (value - y_above)
            + wts[4] * (value - z_below)
            + wts[5] * (value - z_above)
        )

    def stencil_sides(which, inside):
        x_low = jnp.where(first_pln, 0.0, field_x[which, 0].astype(jnp.float32))
        x_high = jnp.where(last_pln, 0.0, field_x[which, 1].astype(jnp.float32))
        z_below = unpack_behind(edge[which + 1, 0])
        z_above = unpack_ahead(edge[which + 1, 1])
        result = (
            inside
            - jnp.where(z_index == 0, wts[4] * z_below, 0.0)
            - jnp.where(z_index == depth - 1, wts[5] * z_above, 0.0)
        )
        top = planes - 1
        if top == 0:
            return result - (wts[0, 0] * x_low + wts[1, 0] * x_high)[None]
        first = result[0] - wts[0, 0] * x_low
        last = result[top] - wts[1, top] * x_high
        return jnp.concatenate([first[None], result[1:top], last[None]], axis=0) if top > 1 else (
            jnp.concatenate([first[None], last[None]], axis=0)
        )

    res_copy.wait()
    for i in range(ZCHUNKS):
        big[i].wait()
        project_some(z, res[...], i * per, (i + 1) * per)
    rhs_part = project_row()
    pl.semaphore_wait(barrier, len(others))
    rows_send(0, rhs_part)
    if turns > 0:
        tokens_send(0)

    lab_copy.wait()
    level_copy.wait()
    narrow = lab[...].astype(jnp.float32)
    lab_send[...] = narrow.astype(jnp.bfloat16)
    edge_send[0] = pack_edges(narrow)
    label_copies = edge_copies(0) + plane_copies(0, lab_send, lab_x)
    for copy in label_copies:
        copy.start()

    @pl.loop(0, modes // 8)
    def _(block):
        for inner in range(8):
            k = block * 8 + inner
            mode = z[k].astype(jnp.float32)
            zf[k] = mode
            edge_modes[k] = pack_edges(mode)

    def density(labels):
        value = jnp.full(labels.shape, levels[0], jnp.float32)
        for i in range(1, levels.shape[0]):
            value = jnp.where(labels == float(i), levels[i], value)
        return value

    rhs = rows_wait(0)
    copies = expand(0, rhs)
    for turn in range(1, turns):
        tokens_wait(turn - 1)
        tokens_send(turn)
    for copy in label_copies:
        copy.wait_recv()
    coef = density(lab[...].astype(jnp.float32))
    low = jnp.where(first_pln, coef[0], density(lab_x[0].astype(jnp.float32)))
    high = jnp.where(last_pln, coef[planes - 1], density(lab_x[1].astype(jnp.float32)))
    wts[0] = harmonic(coef, jnp.concatenate([low[None], coef[:-1]], axis=0))
    wts[1] = harmonic(coef, jnp.concatenate([coef[1:], high[None]], axis=0))
    wts[2] = harmonic(coef, jnp.where(y_index == 0, coef, pltpu.roll(coef, 1, 1)))
    wts[3] = harmonic(
        coef, jnp.where(y_index == height - 1, coef, pltpu.roll(coef, height - 1, 1))
    )
    z_low, z_high = along_z(coef, density(edge[0, 0]), density(edge[0, 1]))
    wts[4] = harmonic(coef, z_low)
    wts[5] = harmonic(coef, z_high)

    inside = stencil_inside(0)
    for copy in copies:
        copy.wait_recv()
    image = stencil_sides(0, inside)
    project_some(zf, image, 0, modes)
    if turns > 0:
        tokens_wait(turns - 1)
    rows_send(1, project_row())

    image_row = rows_wait(1)
    copies = expand(1, image_row)
    dq = across_lanes(rhs * image_row)
    qq = across_lanes(image_row * image_row)
    guess = jnp.where(qq > 0.0, dq / jnp.where(qq > 0.0, qq, 1.0), 0.0)
    rest = rhs - guess * image_row
    shared = {
        RR: across_lanes(rhs * rhs),
        DQ: dq,
        UU: across_lanes(rest * rest),
        UQ: across_lanes(rest * image_row),
        QQ: qq,
    }
    spot = lane - SLOT * place
    packet = jnp.zeros((1, depth), jnp.float32)
    for i, value in shared.items():
        packet = jnp.where(spot == i, jnp.where(first_pln, value, 0.0), packet)
    guesses = jnp.where(
        jnp.logical_and(spot >= 0, spot < SLOT), jnp.where(first_pln, guess, 0.0), 0.0
    )
    inside = stencil_inside(1)
    for copy in copies:
        copy.wait_recv()
    image_next = stencil_sides(1, inside)
    guess3 = guess[:, :, None]
    rest_field = field[0] - guess3 * field[1]
    rest_image = image - guess3 * image_next
    local = {
        S1: whole(rest_field * rest_image),
        S2: whole(rest_field * image_next + field[1] * rest_image),
        S3: whole(field[1] * image_next),
    }
    for i, value in local.items():
        packet = jnp.where(spot == i, value, packet)

    near[near_me] = jnp.concatenate([packet, guesses], axis=0)
    mine = near.at[near_me]
    for peer in near_peers:
        remote(mine, mine, sum_send.at[0], sum_recv.at[0], peer).start()
    both = near.at[pl.ds(0, near_count - 1)]
    pltpu.make_async_copy(both, both, sum_recv.at[0]).wait()
    wide[wide_me] = jnp.sum(near[...], axis=0)
    mine = wide.at[wide_me]
    for peer in wide_peers:
        remote(mine, mine, sum_send.at[1], sum_recv.at[1], peer).start()
    for copy in pending:
        copy.wait_send()
    for which in range(2):
        both = rows.at[which, pl.ds(0, npln - 1)]
        pltpu.make_async_copy(both, both, row_send.at[which]).wait()
    both = near.at[pl.ds(0, near_count - 1)]
    pltpu.make_async_copy(both, both, sum_send.at[0]).wait()

    both = wide.at[pl.ds(0, wide_count - 1)]
    pltpu.make_async_copy(both, both, sum_recv.at[1]).wait()
    count = wide_count // halves
    pairs = []
    for i in range(count):
        pair = wide[i]
        for j in range(1, halves):
            pair = pair + wide[j * count + i]
        pairs.append(pair)
    table = jnp.concatenate(pairs, axis=0)
    shape = table.shape
    upper = lax.broadcasted_iota(jnp.int32, shape, 0) % 2 == 0
    kind = jnp.where(upper, lax.broadcasted_iota(jnp.int32, shape, 1) % SLOT, SLOT)
    step_guess = pltpu.roll(table, shape[0] - 1, 0)

    def total(value):
        return across_lanes(jnp.sum(value, axis=0, keepdims=True))

    norm = total(jnp.where(kind == RR, table, 0.0))
    curve = total(jnp.where(kind == DQ, table, 0.0))
    alpha = norm / curve
    delta = alpha - step_guess
    squared = delta * delta * table
    norm_next = total(
        jnp.where(kind == UU, table, 0.0)
        + jnp.where(kind == UQ, -2.0 * delta * table, 0.0)
        + jnp.where(kind == QQ, squared, 0.0)
    )
    curve_rest = total(
        jnp.where(kind == S1, table, 0.0)
        + jnp.where(kind == S2, -delta * table, 0.0)
        + jnp.where(kind == S3, squared, 0.0)
    )
    mixed = total(
        jnp.where(kind == UQ, table, 0.0) + jnp.where(kind == QQ, -delta * table, 0.0)
    )
    beta = norm_next / norm
    curve_next = curve_rest + 2.0 * beta * mixed + beta * beta * curve
    alpha_next = norm_next / curve_next
    first_part = alpha + alpha_next * (1.0 + beta)
    second_part = alpha_next * alpha
    solution_row = first_part * rhs - second_part * image_row
    sol_ref[...] = solution_row[:, :modes]
    defl_ref[...] = (
        res[...] - first_part[:, :, None] * image + second_part[:, :, None] * image_next
    )

    both = wide.at[pl.ds(0, wide_count - 1)]
    pltpu.make_async_copy(both, both, sum_send.at[1]).wait()


def finish(row, out, sol_hbm, defl_hbm, sems):
    copies = [
        pltpu.make_async_copy(out, defl_hbm, sems.at[0]),
        pltpu.make_async_copy(row, sol_hbm, sems.at[1]),
    ]
    for copy in copies:
        copy.start()
    for copy in copies:
        copy.wait()


def body(sides, labels, levels, zvec, resid):
    modes = zvec.shape[0]
    block = resid.shape
    ny, nz, npln = sides
    lanes = block[-1]
    in_hbm = pl.BlockSpec(memory_space=pltpu.HBM)
    vmem = pl.BlockSpec(memory_space=pltpu.VMEM)
    dma = pltpu.SemaphoreType.DMA
    wide = jnp.float32
    row, out = pl.pallas_call(
        functools.partial(kernel, sides),
        out_shape=(
            jax.ShapeDtypeStruct((1, modes), wide),
            jax.ShapeDtypeStruct(block, wide),
        ),
        in_specs=[in_hbm] * 4,
        out_specs=(vmem, vmem),
        scratch_shapes=[
            pltpu.VMEM(zvec.shape, zvec.dtype),
            pltpu.VMEM(zvec.shape, wide),
            pltpu.VMEM(block, labels.dtype),
            pltpu.VMEM(block, wide),
            pltpu.VMEM(block, jnp.bfloat16),
            pltpu.VMEM((2,) + block[1:], jnp.bfloat16),
            pltpu.VMEM((2,) + block, wide),
            pltpu.VMEM((2,) + block, jnp.bfloat16),
            pltpu.VMEM((2, 2) + block[1:], jnp.bfloat16),
            pltpu.VMEM((3, 8, lanes), wide),
            pltpu.VMEM((3, 2, 8, lanes), wide),
            pltpu.VMEM((modes, 8, lanes), wide),
            pltpu.VMEM((modes, lanes), wide),
            pltpu.VMEM((modes, lanes), wide),
            pltpu.VMEM((2, npln, 1, lanes), wide),
            pltpu.VMEM((4 * ny, 2, lanes), wide),
            pltpu.VMEM((npln // 2 * nz, 2, lanes), wide),
            pltpu.VMEM((6,) + block, wide),
            pltpu.SMEM(levels.shape, wide),
            dma((3 + ZCHUNKS,)),
            dma((3, 8)),
            dma((3, 8)),
            dma((2,)),
            dma((2,)),
            dma((2,)),
            dma((2,)),
            pltpu.SemaphoreType.REGULAR((2, 4)),
        ],
        compiler_params=pltpu.CompilerParams(
            collective_id=0, has_side_effects=True, vmem_limit_bytes=24 << 20
        ),
        name="deflated_coarse",
    )(
        *(pltpu.with_memory_space_constraint(a, pltpu.HBM) for a in (levels, labels, zvec, resid))
    )
    return pl.pallas_call(
        finish,
        out_shape=(
            jax.ShapeDtypeStruct((1, modes), wide),
            jax.ShapeDtypeStruct(block, wide),
        ),
        in_specs=[vmem, vmem],
        out_specs=(in_hbm, in_hbm),
        scratch_shapes=[dma((2,))],
        compiler_params=pltpu.CompilerParams(vmem_limit_bytes=2 << 20),
        name="finish",
    )(row, out)


def solution(mesh):
    chips = mesh.shape["sub"] // 2
    side = math.isqrt(chips)
    sides = (chips // side, side, mesh.shape["pln"])
    in_specs = (P("pln", None, "sub"), P(), P(None, "pln", None, "sub"), P("pln", None, "sub"))
    out_specs = (P("sub", None), P("pln", None, "sub"))
    return jax.shard_map(
        functools.partial(body, sides), mesh=mesh, in_specs=in_specs, out_specs=out_specs,
        check_vma=False,
    )
```
